256 devices in a mesh: tile: 8 (over y, core), plane: 32 (over x, z).
Axes of the slice: x: 4, y: 4, z: 8, core: 2. Of those that a mesh axis runs over, the one named last changes fastest.
Arguments:
- observed: float32 [2, 32, 512, 256], P(None, 'plane', 'tile'), may hold values from 0.5 to 4
- intersection_strip: float32 [2, 32, 256, 256], P(None, 'plane', 'tile'), may hold values from 0.5 to 4
- axial_taps: float32 [2, 41], replicated, may hold values from 0.05 to 1
- lateral_taps: float32 [2, 15], replicated, may hold values from 0.05 to 1
- extents: int32 [8], P('tile'), may hold values from 1 to 32, as said below
- section_skews: int32 [8], P('tile'), may hold values from 0 to 255
Outputs:
- estimate: float32 [2, 32, 512, 256], P(None, 'plane', 'tile')
The draws below stay inside these ranges and needn't reach their ends.
Inputs may be any that keep to these rules, and one draw needn't show every extreme that they name: `extents`: entry 0 is not used; the largest of the entries 1 to 7 is 32.
All inputs are finite; a program needn't handle non-finite values.
Results may differ from the reference program's by a relative error of at most 0.00005.
Values sent between devices are 32-bit elements; how exact they have to be, the bound alone decides.
A program may use at most 64 MiB of HBM per device.

```python
import math
import jax
import jax.numpy as jnp
from jax import lax

CH = 2
KZ = 41
KL = 15
ITERS = 2
YD = 64
NX = 256
MAXOV = 32
TILES = 8
NZ = 32
NY = 512


def draw_extents(key, part):
    first_key, second_key = jax.random.split(jax.random.fold_in(key, 17))
    values = jax.random.randint(first_key, (TILES,), 1, MAXOV + 1)
    chosen = jax.random.randint(second_key, (), 1, TILES)
    return jnp.where(jnp.arange(TILES) == chosen, MAXOV, values).astype(jnp.int32)


def touch_ends(array, own_key, low, high):
    longest = array.shape.index(max(array.shape))
    spots = []
    for shift in (0, 1):
        where = [jax.random.randint(jax.random.fold_in(own_key, axis), (), 0, length) for axis, length in enumerate(array.shape)]
        where[longest] = (where[longest] + shift) % array.shape[longest]
        spots.append(tuple(where))
    return array.at[spots[0]].set(low).at[spots[1]].set(high)


def block_scale(key, dims, cuts, smallest, high):
    gain = 1.0
    for axis_at, shards_of in cuts:
        steps = jax.random.uniform(jax.random.fold_in(jax.random.fold_in(key, 6), axis_at), (shards_of,), jnp.float32, smallest / len(cuts), high / len(cuts))
        gain = gain * jnp.repeat(jnp.exp(steps), dims[axis_at] // shards_of).reshape((-1,) + (1,) * (len(dims) - 1 - axis_at))
    return gain


def setup_inputs(seed: int = 0) -> dict:
    key_of = jax.random.split(jax.random.key(seed), 7)
    return {
        "observed": jnp.clip(jnp.exp(math.log(4.0) - 2.0794415 * jax.random.uniform(key_of[0], (CH, NZ, NY, NX), jnp.float32) ** block_scale(key_of[0], (CH, NZ, NY, NX), ((1, 32), (2, 8)), -0.2, 0.2)), 0.5, 4.0),
        "intersection_strip": jnp.clip(jnp.exp(math.log(4.0) - 2.0794415 * jax.random.uniform(key_of[1], (CH, NZ, TILES * MAXOV, NX), jnp.float32) ** block_scale(key_of[1], (CH, NZ, TILES * MAXOV, NX), ((1, 32), (2, 8)), -0.2, 0.2)), 0.5, 4.0),
        "axial_taps": jnp.clip(jnp.exp(jax.random.uniform(key_of[2], (CH, KZ), jnp.float32, math.log(0.05), math.log(1.0))), 0.05, 1.0),
        "lateral_taps": jnp.clip(jnp.exp(jax.random.uniform(key_of[3], (CH, KL), jnp.float32, math.log(0.05), math.log(1.0))), 0.05, 1.0),
        "extents": draw_extents(jax.random.fold_in(key_of[6], 71), 0),
        "section_skews": touch_ends(jax.random.randint(key_of[5], (TILES,), 0, NX), jax.random.fold_in(key_of[5], 1), 0, NX - 1).astype(jnp.int32),
    }


def shifted_blur(volume, kernel, axis):
    tap_count = kernel.shape[0]
    half_width = tap_count // 2
    padding = [(0, 0)] * volume.ndim
    padding[axis] = (half_width, half_width)
    padded = jnp.pad(volume, padding)
    length_here = volume.shape[axis]
    running = jnp.zeros_like(volume)
    for tap_index in range(tap_count):
        running = running + kernel[tap_index] * lax.slice_in_dim(padded, tap_index, tap_index + length_here, axis=axis)
    return running


def one_channel(operands):
    joined_obs, axial_kernel, lateral_kernel = operands
    axial_flip = jnp.flip(axial_kernel)
    lateral_flip = jnp.flip(lateral_kernel)
    estimate = joined_obs
    for sweep in range(ITERS):
        blurred = shifted_blur(shifted_blur(shifted_blur(estimate, lateral_kernel, 2), lateral_kernel, 1), axial_kernel, 0)
        quotient = joined_obs / blurred
        spread_back = shifted_blur(shifted_blur(shifted_blur(quotient, axial_flip, 0), lateral_flip, 1), lateral_flip, 2)
        estimate = estimate * spread_back
    return estimate


def reference(observed, intersection_strip, axial_taps, lateral_taps, extents, section_skews):
    joined_obs = observed
    for tile_index in range(1, TILES):
        strip_part = intersection_strip[:, :, (tile_index - 1) * MAXOV:tile_index * MAXOV, :]
        strip_part = jnp.roll(strip_part, section_skews[tile_index], axis=3)
        top_rows = observed[:, :, tile_index * YD:tile_index * YD + MAXOV, :]
        inside = (jnp.arange(MAXOV, dtype=jnp.int32) < extents[tile_index])[None, None, :, None]
        blended = jnp.where(inside, 0.5 * (top_rows + strip_part), top_rows)
        joined_obs = joined_obs.at[:, :, tile_index * YD:tile_index * YD + MAXOV, :].set(blended)
    return lax.map(one_channel, (joined_obs, axial_taps, lateral_taps))
```

```python
import functools

import jax
import jax.numpy as jnp
from jax import lax
from jax.experimental import pallas as pl
from jax.experimental.pallas import tpu as pltpu
from jax.sharding import PartitionSpec as P

F32 = jnp.float32
BF16 = jnp.bfloat16
MESH = pl.DeviceIdType.MESH
TILES, PLANES, ITERS = 8, 32, 2
KZ, KL = 41, 15


def pack_to_x(chan, half, tile):
    return 2 * ((chan + half * (tile % 2)) % 2) + half


def split(value):
    high = value.astype(BF16)
    return high, (value - high.astype(F32)).astype(BF16)


def lanes_of(shape):
    return lax.broadcasted_iota(jnp.int32, shape, len(shape) - 1)


def turn(value, by):
    by = by % 128
    return value if by == 0 else pltpu.roll(value, by, value.ndim - 1)


def build_lateral(taps, xt, out):
    lane = lanes_of((32, 128))
    row = lax.broadcasted_iota(jnp.int32, (32, 128), 0)
    x_out, y_out = lane % 32, lane // 32
    side, at = row // 8, row % 8
    own_diff = row - x_out + 7
    left = at - 8 - x_out + 7
    right = at + 32 - x_out + 7
    halo_diff = jnp.where((side == 0) & (xt > 0), left, -1)
    halo_diff = jnp.where((side == 3) & (xt < 7), right, halo_diff)
    blocks = []
    for diff in (own_diff, halo_diff):
        block = jnp.zeros((32, 128), F32)
        for j in range(KL):
            block = jnp.where(diff == j, taps[j], block)
        blocks.append(block)
    for d in range(5):
        for y_in in range(4):
            line = jnp.zeros((32, 128), F32)
            for y in range(4):
                k = 4 * (d - 2) + y_in - y + 7
                if 0 <= k < KL:
                    line = jnp.where(y_out == y, taps[k], line)
            for b, block in enumerate(blocks):
                high, low = split(block * line)
                rows = pl.ds(d * 256 + b * 128 + y_in * 32, 32)
                out[rows, 0:128] = high
                out[rows, 128:256] = low


def build_axial(taps, out):
    lane = lanes_of((32, 128))
    row = lax.broadcasted_iota(jnp.int32, (32, 128), 0)
    diff = lane % 32 - row + KZ // 2
    matrix = jnp.zeros((32, 128), F32)
    for j in range(KZ):
        matrix = jnp.where(diff == j, taps[j], matrix)
    high = matrix.astype(BF16).astype(F32)
    both = jnp.where(lane < 64, high, jnp.where(lane < 96, matrix - high, 0.0))
    out[...] = both.astype(BF16)


def kernel(
    observed, strip, axial, lateral, extents, skews, result,
    obs_v, strip_v, tx, rx, own, sl, sr, hl, hr, yh, ehi, elo, wf, wa, zf, za, ot, ox, res,
    obs_sem, strip_send, strip_recv, in_send, in_recv, halo_send, halo_recv, out_send, out_recv, res_sem,
):
    t = lax.axis_index("tile")
    p = lax.axis_index("plane")
    px, xt = p // 8, p % 8
    h = px % 2
    c = (px // 2 + h * (t % 2)) % 2
    slot = c * 16 + h * 8 + xt
    rr = 2 * t + h

    loads = []
    for ch in range(2):
        for half in range(2):
            loads.append(
                pltpu.make_async_copy(
                    observed.at[ch, 0, :, pl.ds(half * 128, 128)],
                    obs_v.at[pl.ds((ch * 2 + half) * 64, 64), :],
                    obs_sem.at[ch * 2 + half],
                )
            )
    for load in loads:
        load.start()

    def neighbour(dy, dx):
        there = (rr + dy + 2 * TILES) % (2 * TILES)
        tt, hh = there // 2, there % 2
        return {"tile": tt, "plane": pack_to_x(c, hh, tt) * 8 + (xt + dx + 8) % 8}

    barrier = pltpu.get_barrier_semaphore()

    def greet(i, _):
        pl.semaphore_signal(
            barrier, inc=1, device_id={"tile": t, "plane": (p + i) % PLANES}, device_id_type=MESH
        )
        return 0

    lax.fori_loop(1, PLANES, greet, 0)
    outward = jnp.where(h == 0, -1, 1)
    for dx in (-1, 0, 1):
        pl.semaphore_signal(barrier, inc=1, device_id=neighbour(outward, dx), device_id_type=MESH)
    after = {"tile": (t + 1) % TILES, "plane": p}
    before = {"tile": (t + TILES - 1) % TILES, "plane": p}
    for other in (after, before):
        pl.semaphore_signal(barrier, inc=1, device_id=other, device_id_type=MESH)
    pl.semaphore_wait(barrier, PLANES - 1 + 5)

    strips = []
    for ch in range(2):
        for half in range(2):
            strips.append(
                pltpu.make_async_remote_copy(
                    src_ref=strip.at[ch, 0, :, pl.ds(half * 128, 128)],
                    dst_ref=strip_v.at[pl.ds((ch * 2 + half) * 32, 32), :],
                    send_sem=strip_send.at[ch * 2 + half],
                    recv_sem=strip_recv.at[ch * 2 + half],
                    device_id=after,
                    device_id_type=MESH,
                )
            )
    for copy in strips:
        copy.start()
    for load in loads:
        load.wait()

    lane = lanes_of((8, 128))
    group = lane // 32

    def to_blocks(hh):
        for ch in range(2):
            for half in range(2):
                base = (ch * 2 + half) * 64 + hh * 32
                rows = [obs_v[pl.ds(base + y, 8, stride=4), :] for y in range(4)]
                for q in range(4):
                    tile = turn(rows[0], 32 * (0 - q))
                    for y in range(1, 4):
                        tile = jnp.where(group == y, turn(rows[y], 32 * (y - q)), tile)
                    tx[ch * 16 + hh * 8 + half * 4 + q] = tile

        def send(i, _):
            ch, xx = i // 8, (i + xt) % 8
            to = pack_to_x(ch, hh, t) * 8 + xx

            @pl.when(to != p)
            def _():
                pltpu.make_async_remote_copy(
                    src_ref=tx.at[ch * 16 + hh * 8 + xx],
                    dst_ref=rx.at[pl.ds(pl.multiple_of(p * 8, 8), 8), :],
                    send_sem=in_send,
                    recv_sem=in_recv,
                    device_id={"tile": t, "plane": to},
                    device_id_type=MESH,
                ).start()

            return 0

        lax.fori_loop(0, 16, send, 0)

    to_blocks(1)

    lat = [lateral[c, j] for j in range(KL)]
    ax = [axial[c, j] for j in range(KZ)]
    build_axial(ax, zf)
    build_lateral(lat, xt, wf)

    for copy in strips:
        copy.wait_recv()
    reach = jnp.where(t == 0, 0, extents[0])
    skew = skews[0]
    shift = skew % 128
    wide_lane = lanes_of((32, 128))
    inside = lax.broadcasted_iota(jnp.int32, (32, 128), 0) < reach
    for ch in range(2):
        low = strip_v[pl.ds(ch * 64, 32), :]
        high = strip_v[pl.ds(ch * 64 + 32, 32), :]
        low = pltpu.roll(low, shift, 1)
        high = pltpu.roll(high, shift, 1)
        wrapped = wide_lane < shift
        first = jnp.where(wrapped, high, low)
        second = jnp.where(wrapped, low, high)
        far = skew >= 128
        for half in range(2):
            moved = jnp.where(far, (second, first)[half], (first, second)[half])
            rows = pl.ds((ch * 2 + half) * 64, 32)
            top = obs_v[rows, :]
            obs_v[rows, :] = jnp.where(inside, 0.5 * (top + moved), top)
    to_blocks(0)
    rx[pl.ds(pl.multiple_of(p * 8, 8), 8), :] = tx[slot]

    build_axial(ax[::-1], za)
    build_lateral(lat[::-1], xt, wa)

    most = pl.ds(0, (PLANES - 1) * 8)
    pltpu.make_async_copy(rx.at[most, :], rx.at[most, :], in_recv).wait()
    joined = jnp.concatenate([rx[pl.ds(ys, 32, stride=8), :][None] for ys in range(8)], axis=0)

    edge = (lanes_of((8, 8, 128)) // 8) % 4
    edge12 = (lanes_of((12, 8, 128)) // 8) % 4
    row12 = lax.broadcasted_iota(jnp.int32, (12, 8, 128), 0)
    live12 = ((row12 >= 2) | (rr > 0)) & ((row12 < 10) | (rr < 2 * TILES - 1))

    def spread(value, w, z, n):
        own[n] = value
        parts = [value[:, 8 * k : 8 * k + 8, :] for k in range(4)]
        to_right = turn(parts[0], -24)
        to_left = parts[0]
        for k in range(1, 4):
            to_right = jnp.where(edge == k, turn(parts[k], 8 * k - 24), to_right)
            to_left = jnp.where(edge == k, turn(parts[k], 8 * k), to_left)
        sr[n] = to_right
        sl[n] = to_left
        copies = []
        for dx, source, target, sem in ((1, sr, hl, 0), (-1, sl, hr, 1)):
            for dy, rows, size, at in ((-1, 0, 2, 10), (0, 0, 8, 2), (1, 6, 2, 0)):
                copies.append((source.at[n, pl.ds(rows, size)], target.at[n, pl.ds(at, size)], sem, neighbour(dy, dx)))
        for dy, rows, at in ((-1, 0, 1), (1, 6, 0)):
            copies.append((own.at[n, pl.ds(rows, 2)], yh.at[n, at], 2, neighbour(dy, 0)))
        for source, target, sem, to in copies:
            pltpu.make_async_remote_copy(
                src_ref=source,
                dst_ref=target,
                send_sem=halo_send.at[n, sem],
                recv_sem=halo_recv.at[n, sem],
                device_id=to,
                device_id_type=MESH,
            ).start()
        ehi[2:10, :, 0:128], elo[2:10, :, 0:128] = split(value)
        pltpu.make_async_copy(yh.at[n], yh.at[n], halo_recv.at[n, 2]).wait()
        ehi[0:2, :, 0:128], elo[0:2, :, 0:128] = split(jnp.where(rr > 0, yh[n, 0], 0.0))
        ehi[10:12, :, 0:128], elo[10:12, :, 0:128] = split(jnp.where(rr < 2 * TILES - 1, yh[n, 1], 0.0))
        pltpu.make_async_copy(hl.at[n], hl.at[n], halo_recv.at[n, 0]).wait()
        pltpu.make_async_copy(hr.at[n], hr.at[n], halo_recv.at[n, 1]).wait()
        left = jnp.where(live12, hl[n], 0.0)
        right = jnp.where(live12, hr[n], 0.0)
        sides = [jnp.where(edge12 < 2, turn(left, -8 * k), turn(right, 24 - 8 * k)) for k in range(4)]
        ehi[:, :, 128:256], elo[:, :, 128:256] = split(jnp.concatenate(sides, axis=1))
        high = jnp.concatenate([ehi[d : d + 8].reshape(256, 256) for d in range(5)], axis=1)
        low = jnp.concatenate([elo[d : d + 8].reshape(256, 256) for d in range(5)], axis=1)
        both = jnp.dot(high, w[...], preferred_element_type=F32)
        flat = both[:, 0:128] + both[:, 128:256]
        flat = flat + jnp.dot(low, w[:, 0:128], preferred_element_type=F32)
        high, low = split(flat.reshape(8, 32, 128))
        stacked = jnp.concatenate([high, low, high], axis=1)
        wide = jnp.concatenate([stacked[ys] for ys in range(8)], axis=1)
        done = jnp.dot(z[:, 0:96], wide, preferred_element_type=F32)
        return jnp.concatenate([done[:, 128 * ys : 128 * ys + 128][None] for ys in range(8)], axis=0)

    estimate = joined
    for sweep in range(ITERS):
        blurred = spread(estimate, wf, zf, 2 * sweep)
        quotient = joined / blurred
        estimate = estimate * spread(quotient, wa, za, 2 * sweep + 1)

    for ys in range(8):
        ot[pl.ds(ys, 32, stride=8), :] = estimate[ys]

    def send_back(i, _):
        to = (p + i) % PLANES
        pltpu.make_async_remote_copy(
            src_ref=ot.at[pl.ds(pl.multiple_of(to * 8, 8), 8), :],
            dst_ref=ox.at[slot],
            send_sem=out_send,
            recv_sem=out_recv,
            device_id={"tile": t, "plane": to},
            device_id_type=MESH,
        ).start()
        return 0

    lax.fori_loop(1, PLANES, send_back, 0)
    ox[slot] = ot[pl.ds(pl.multiple_of(p * 8, 8), 8), :]
    few = pl.ds(0, PLANES - 1)
    pltpu.make_async_copy(ox.at[few], ox.at[few], out_recv).wait()
    stores = []
    for ch in range(2):
        for half in range(2):
            for hh in range(2):
                tiles = [ox[ch * 16 + hh * 8 + half * 4 + q] for q in range(4)]
                for y in range(4):
                    line = turn(tiles[0], 32 * (0 - y))
                    for q in range(1, 4):
                        line = jnp.where(group == q, turn(tiles[q], 32 * (q - y)), line)
                    res[pl.ds((ch * 2 + half) * 64 + hh * 32 + y, 8, stride=4), :] = line
            store = pltpu.make_async_copy(
                res.at[pl.ds((ch * 2 + half) * 64, 64), :],
                result.at[ch, 0, :, pl.ds(half * 128, 128)],
                res_sem.at[ch * 2 + half],
            )
            store.start()
            stores.append(store)

    for copy in strips:
        copy.wait_send()
    pltpu.make_async_copy(tx.at[few], tx.at[few], in_send).wait()
    for n in range(2 * ITERS):
        pltpu.make_async_copy(hl.at[n], hl.at[n], halo_send.at[n, 0]).wait()
        pltpu.make_async_copy(hr.at[n], hr.at[n], halo_send.at[n, 1]).wait()
        pltpu.make_async_copy(yh.at[n], yh.at[n], halo_send.at[n, 2]).wait()
    pltpu.make_async_copy(ox.at[few], ox.at[few], out_send).wait()
    for store in stores:
        store.wait()


def shards(observed, intersection_strip, axial_taps, lateral_taps, extents, section_skews):
    anywhere = pl.BlockSpec(memory_space=pl.ANY)
    scalars = pl.BlockSpec(memory_space=pltpu.SMEM)
    rounds = 2 * ITERS
    dma = pltpu.SemaphoreType.DMA
    return pl.pallas_call(
        kernel,
        out_shape=jax.ShapeDtypeStruct(observed.shape, F32),
        in_specs=[anywhere, anywhere, scalars, scalars, scalars, scalars],
        out_specs=anywhere,
        scratch_shapes=[
            pltpu.VMEM((256, 128), F32),
            pltpu.VMEM((128, 128), F32),
            pltpu.VMEM((32, 8, 128), F32),
            pltpu.VMEM((256, 128), F32),
            pltpu.VMEM((rounds, 8, 32, 128), F32),
            pltpu.VMEM((rounds, 8, 8, 128), F32),
            pltpu.VMEM((rounds, 8, 8, 128), F32),
            pltpu.VMEM((rounds, 12, 8, 128), F32),
            pltpu.VMEM((rounds, 12, 8, 128), F32),
            pltpu.VMEM((rounds, 2, 2, 32, 128), F32),
            pltpu.VMEM((12, 32, 256), BF16),
            pltpu.VMEM((12, 32, 256), BF16),
            pltpu.VMEM((1280, 256), BF16),
            pltpu.VMEM((1280, 256), BF16),
            pltpu.VMEM((32, 128), BF16),
            pltpu.VMEM((32, 128), BF16),
            pltpu.VMEM((256, 128), F32),
            pltpu.VMEM((32, 8, 128), F32),
            pltpu.VMEM((256, 128), F32),
            dma((4,)),
            dma((4,)),
            dma((4,)),
            dma,
            dma,
            dma((rounds, 3)),
            dma((rounds, 3)),
            dma,
            dma,
            dma((4,)),
        ],
        compiler_params=pltpu.CompilerParams(collective_id=0, has_side_effects=True),
        name="richardson_lucy",
    )(observed, intersection_strip, axial_taps, lateral_taps, extents, section_skews)


def solution(mesh):
    in_specs = (
        P(None, "plane", "tile", None),
        P(None, "plane", "tile", None),
        P(),
        P(),
        P("tile"),
        P("tile"),
    )
    out_specs = P(None, "plane", "tile", None)
    return jax.shard_map(shards, mesh=mesh, in_specs=in_specs, out_specs=out_specs, check_vma=False)
```

```python
import jax
import jax.numpy as jnp
from jax import lax
from jax.experimental import pallas as pl
from jax.experimental.pallas import tpu as pltpu
from jax.sharding import PartitionSpec as P

F32 = jnp.float32
BF16 = jnp.bfloat16
MESH = pl.DeviceIdType.MESH
TILES, PLANES, ITERS = 8, 32, 2
KZ, KL = 41, 15


def home_of(chan, row, xt):
    y, turn_x, q = row // 4, row % 4, xt // 2
    px = jnp.where(y % 2 == 0, turn_x, 3 - turn_x)
    return {"tile": 2 * y + (xt + q) % 2, "plane": 8 * px + 4 * chan + q}


def split(value):
    high = value.astype(BF16)
    return high, (value - high.astype(F32)).astype(BF16)


def lanes_of(shape):
    return lax.broadcasted_iota(jnp.int32, shape, len(shape) - 1)


def turn(value, by):
    by = by % 128
    return value if by == 0 else pltpu.roll(value, by, value.ndim - 1)


def build_lateral(taps, out):
    lane = lanes_of((32, 128))
    row = lax.broadcasted_iota(jnp.int32, (32, 128), 0)
    x_out, y_out = lane % 32, lane // 32
    side, at = row // 8, row % 8
    own_diff = row - x_out + 7
    left = at - 8 - x_out + 7
    right = at + 32 - x_out + 7
    halo_diff = jnp.where(side == 0, left, jnp.where(side == 3, right, -1))
    blocks = []
    for diff in (own_diff, halo_diff):
        block = jnp.zeros((32, 128), F32)
        for j in range(KL):
            block = jnp.where(diff == j, taps[j], block)
        blocks.append(block)
    for d in range(5):
        for y_in in range(4):
            line = jnp.zeros((32, 128), F32)
            for y in range(4):
                k = 4 * (d - 2) + y_in - y + 7
                if 0 <= k < KL:
                    line = jnp.where(y_out == y, taps[k], line)
            for b, block in enumerate(blocks):
                high, low = split(block * line)
                rows = pl.ds(b * 640 + d * 128 + y_in * 32, 32)
                out[rows, 0:128] = high
                out[rows, 128:256] = low


def build_axial(taps, out):
    lane = lanes_of((32, 128))
    row = lax.broadcasted_iota(jnp.int32, (32, 128), 0)
    diff = lane % 32 - row + KZ // 2
    matrix = jnp.zeros((32, 128), F32)
    for j in range(KZ):
        matrix = jnp.where(diff == j, taps[j], matrix)
    high = matrix.astype(BF16).astype(F32)
    both = jnp.where(lane < 64, high, jnp.where(lane < 96, matrix - high, 0.0))
    out[...] = both.astype(BF16)


def far_first(i):
    return 4 + ((i + 1) // 2) * (1 - 2 * (i % 2))


def kernel(
    observed, strip, axial, lateral, extents, skews, ox,
    obs_v, strip_s, strip_v, tx, rx, own, sl, sr, hl, hr, yh, eo, eh, wf, wa, zf, za, ot,
    obs_sem, strip_load, strip_send, strip_recv, in_send, in_recv, halo_send, halo_recv, out_send, out_recv,
):
    t = lax.axis_index("tile")
    p = lax.axis_index("plane")
    px, pz = p // 8, p % 8
    y, core = t // 2, t % 2
    c, q_own = pz // 4, pz % 4
    xt = 2 * q_own + (core + q_own) % 2
    rr = 4 * y + jnp.where(y % 2 == 0, px, 3 - px)
    h = rr % 2
    source = rr // 2
    slot = c * 16 + h * 8 + xt
    at_home = source == t

    loads = []
    strip_loads = []
    for ch in range(2):
        for half in range(2):
            i = ch * 2 + half
            lanes = pl.ds(half * 128, 128)
            strip_loads.append(
                pltpu.make_async_copy(strip.at[ch, 0, :, lanes], strip_s.at[pl.ds(i * 32, 32), :], strip_load.at[i])
            )
            loads.append(
                pltpu.make_async_copy(observed.at[ch, 0, :, lanes], obs_v.at[pl.ds(i * 64, 64), :], obs_sem.at[i])
            )
    for load in strip_loads + loads:
        load.start()

    strip_v[...] = jnp.zeros(strip_v.shape, F32)
    hl[...] = jnp.zeros(hl.shape, F32)
    hr[...] = jnp.zeros(hr.shape, F32)
    yh[...] = jnp.zeros(yh.shape, F32)

    def exists(dy, dx):
        fine = (xt + dx >= 0) & (xt + dx < 8)
        return fine & (rr + dy >= 0) & (rr + dy < 2 * TILES)

    around = [(dy, dx) for dy in (-1, 1) for dx in (-1, 1)] + [(0, -1), (0, 1), (-1, 0), (1, 0)]
    after = {"tile": t + 1, "plane": p}
    before = {"tile": t - 1, "plane": p}

    barrier = pltpu.get_barrier_semaphore()

    def greet(to):
        pl.semaphore_signal(barrier, inc=1, device_id=to, device_id_type=MESH)

    def greet_blocks(i, _):
        zz = (pz + far_first(i)) % 8
        for hh in range(2):
            for cc in range(2):
                to = home_of(zz // 4, 2 * t + hh, 2 * (zz % 4) + cc)

                @pl.when((to["plane"] != p) | (to["tile"] != t))
                def _():
                    greet(to)

        low = jnp.where((core + y) % 2 == 0, 2, 0)
        for xx in range(2):
            greet({"tile": source, "plane": 8 * (low + xx) + zz})
        return 0

    lax.fori_loop(0, 8, greet_blocks, 0)
    met = 48 - jnp.where(at_home, 1, 0)
    for dy, dx in around:

        @pl.when(exists(dy, dx))
        def _():
            greet(home_of(c, rr + dy, xt + dx))

        met = met + jnp.where(exists(dy, dx), 1, 0)

    @pl.when(t < TILES - 1)
    def _():
        greet(after)

    @pl.when(t > 0)
    def _():
        greet(before)

    met = met + jnp.where(t < TILES - 1, 1, 0) + jnp.where(t > 0, 1, 0)

    lane = lanes_of((8, 128))
    group = lane // 32

    def to_blocks(hh):
        for ch in range(2):
            for half in range(2):
                base = (ch * 2 + half) * 64 + hh * 32
                rows = [obs_v[pl.ds(base + y, 8, stride=4), :] for y in range(4)]
                for q in range(4):
                    tile = turn(rows[0], 32 * (0 - q))
                    for y in range(1, 4):
                        tile = jnp.where(group == y, turn(rows[y], 32 * (y - q)), tile)
                    tx[ch * 16 + hh * 8 + half * 4 + q] = tile

    def send_blocks(hh):
        def send(i, _):
            zz = (pz + far_first(i)) % 8
            for cc in range(2):
                xx = 2 * (zz % 4) + cc
                to = home_of(zz // 4, 2 * t + hh, xx)

                @pl.when((to["plane"] != p) | (to["tile"] != t))
                def _():
                    pltpu.make_async_remote_copy(
                        src_ref=tx.at[(zz // 4) * 16 + hh * 8 + xx],
                        dst_ref=rx.at[pl.ds(pl.multiple_of(p * 8, 8), 8), :],
                        send_sem=in_send,
                        recv_sem=in_recv,
                        device_id=to,
                        device_id_type=MESH,
                    ).start()

            return 0

        lax.fori_loop(0, 8, send, 0)

    for load in loads + strip_loads:
        load.wait()
    to_blocks(1)
    pl.semaphore_wait(barrier, met)

    strips = []
    for i in range(4):
        rows = pl.ds(i * 32, 32)
        strips.append(
            pltpu.make_async_remote_copy(
                src_ref=strip_s.at[rows, :],
                dst_ref=strip_v.at[rows, :],
                send_sem=strip_send.at[i],
                recv_sem=strip_recv.at[i],
                device_id=after,
                device_id_type=MESH,
            )
        )

    @pl.when(t < TILES - 1)
    def _():
        for copy in strips:
            copy.start()

    send_blocks(1)

    lat = [lateral[c, j] for j in range(KL)]
    ax = [axial[c, j] for j in range(KZ)]
    build_axial(ax, zf)
    build_lateral(lat, wf)
    eo[...] = jnp.zeros(eo.shape, BF16)
    eh[...] = jnp.zeros(eh.shape, BF16)

    @pl.when(t > 0)
    def _():
        for copy in strips:
            copy.wait_recv()

    reach = jnp.where(t == 0, 0, extents[0])
    skew = skews[0]
    shift = skew % 128
    wide_lane = lanes_of((32, 128))
    inside = lax.broadcasted_iota(jnp.int32, (32, 128), 0) < reach
    for ch in range(2):
        low = strip_v[pl.ds(ch * 64, 32), :]
        high = strip_v[pl.ds(ch * 64 + 32, 32), :]
        low = pltpu.roll(low, shift, 1)
        high = pltpu.roll(high, shift, 1)
        wrapped = wide_lane < shift
        first = jnp.where(wrapped, high, low)
        second = jnp.where(wrapped, low, high)
        far = skew >= 128
        for half in range(2):
            moved = jnp.where(far, (second, first)[half], (first, second)[half])
            rows = pl.ds((ch * 2 + half) * 64, 32)
            top = obs_v[rows, :]
            obs_v[rows, :] = jnp.where(inside, 0.5 * (top + moved), top)
    to_blocks(0)
    send_blocks(0)

    @pl.when(at_home)
    def _():
        rx[pl.ds(pl.multiple_of(p * 8, 8), 8), :] = tx[slot]

    build_axial(ax[::-1], za)
    build_lateral(lat[::-1], wa)

    @pl.when(at_home)
    def _():
        most = pl.ds(0, (PLANES - 1) * 8)
        pltpu.make_async_copy(rx.at[most, :], rx.at[most, :], in_recv).wait()

    @pl.when(jnp.logical_not(at_home))
    def _():
        pltpu.make_async_copy(rx, rx, in_recv).wait()

    joined = jnp.concatenate([rx[pl.ds(ys, 32, stride=8), :][None] for ys in range(8)], axis=0)

    edge = (lanes_of((8, 8, 128)) // 8) % 4
    edge2 = (lanes_of((2, 8, 128)) // 8) % 4
    sent = []

    def banded(high, low, w, first, last):
        both = jnp.dot(high, w[first:last, :], preferred_element_type=F32)
        more = jnp.dot(low, w[first:last, 0:128], preferred_element_type=F32)
        return both[:, 0:128] + both[:, 128:256] + more

    def along_z(flat, z):
        n = flat.shape[0] // 32
        high, low = split(flat.reshape(n, 32, 128))
        stacked = jnp.concatenate([high, low, high], axis=1)
        wide = jnp.concatenate([stacked[i] for i in range(n)], axis=1)
        done = jnp.dot(z[:, 0:96], wide, preferred_element_type=F32)
        return [done[:, 128 * i : 128 * i + 128] for i in range(n)]

    def shifted(pad, value, w, base):
        pad[0, 2:10], pad[1, 2:10] = split(value)
        wide = [jnp.concatenate([pad[s, d : d + 8].reshape(256, 128) for d in range(5)], axis=1) for s in range(2)]
        return banded(wide[0], wide[1], w, base, base + 640)

    def unpack(left, right, which):
        sides = [jnp.where(which < 2, turn(left, -8 * k), turn(right, 24 - 8 * k)) for k in range(4)]
        return jnp.concatenate(sides, axis=1)

    def spread(value, w, z, n):
        own[n] = value
        parts = [value[:, 8 * k : 8 * k + 8, :] for k in range(4)]
        to_right = turn(parts[0], -24)
        to_left = parts[0]
        for k in range(1, 4):
            to_right = jnp.where(edge == k, turn(parts[k], 8 * k - 24), to_right)
            to_left = jnp.where(edge == k, turn(parts[k], 8 * k), to_left)
        sr[n] = to_right
        sl[n] = to_left
        copies = {}
        for i, (dy, dx) in enumerate(around):
            rows, size, at = {-1: (0, 2, 10), 0: (0, 8, 2), 1: (6, 2, 0)}[dy]
            if dx == 0:
                src, dst = own.at[n, pl.ds(rows, 2)], yh.at[n, 0 if dy == 1 else 1]
            else:
                src = (sr if dx == 1 else sl).at[n, pl.ds(rows, size)]
                dst = (hl if dx == 1 else hr).at[n, pl.ds(at, size)]
            copy = pltpu.make_async_remote_copy(
                src_ref=src,
                dst_ref=dst,
                send_sem=halo_send.at[n, i],
                recv_sem=halo_recv.at[n, i],
                device_id=home_of(c, rr + dy, xt + dx),
                device_id_type=MESH,
            )
            copies[dy, dx] = copy

            @pl.when(exists(dy, dx))
            def _():
                copy.start()

            sent.append((exists(dy, dx), copy))

        def arrive(dy, dx):
            @pl.when(exists(-dy, -dx))
            def _():
                copies[dy, dx].wait_recv()

        whole = along_z(shifted(eo, value, w, 0), z)
        arrive(0, 1)
        arrive(0, -1)
        beside = unpack(hl[n, 2:10], hr[n, 2:10], edge)
        sides = along_z(shifted(eh, beside, w, 640), z)
        whole = [a + b for a, b in zip(whole, sides)]
        for dy, dx in around:
            if dy != 0:
                arrive(dy, dx)
        ends = []
        for at, rows in ((0, 0), (1, 10)):
            corner = unpack(hl[n, rows : rows + 2], hr[n, rows : rows + 2], edge2)
            ends.append([split(yh[n, at]), split(corner)])
        flat = []
        for at in range(2):
            total = None
            for b in range(2):
                wide = []
                for s in range(2):
                    pair = ends[at][b][s]
                    none = jnp.zeros((32, 128), BF16)
                    if at == 0:
                        lines = ((pair[0], pair[1]), (pair[1], none))
                    else:
                        lines = ((none, pair[0]), (pair[0], pair[1]))
                    wide.append(jnp.concatenate([jnp.concatenate(line, axis=1) for line in lines], axis=0))
                first = b * 640 + (0 if at == 0 else 3 * 128)
                part = banded(wide[0], wide[1], w, first, first + 256)
                total = part if total is None else total + part
            flat.append(total)
        outer = along_z(jnp.concatenate(flat, axis=0), z)
        for i, ys in enumerate((0, 1, 6, 7)):
            whole[ys] = whole[ys] + outer[i]
        return jnp.concatenate([line[None] for line in whole], axis=0)

    estimate = joined
    for sweep in range(ITERS):
        blurred = spread(estimate, wf, zf, 2 * sweep)
        quotient = joined / blurred
        estimate = estimate * spread(quotient, wa, za, 2 * sweep + 1)

    for ys in range(8):
        ot[pl.ds(ys, 32, stride=8), :] = estimate[ys]

    def send_back(i, _):
        zz = (pz + far_first(i)) % 8
        for dx in (2, 1, 3, 0):
            to = 8 * ((px + dx) % 4) + zz

            @pl.when((to != p) | jnp.logical_not(at_home))
            def _():
                pltpu.make_async_remote_copy(
                    src_ref=ot.at[pl.ds(pl.multiple_of(to * 8, 8), 8), :],
                    dst_ref=ox.at[slot],
                    send_sem=out_send,
                    recv_sem=out_recv,
                    device_id={"tile": source, "plane": to},
                    device_id_type=MESH,
                ).start()

        return 0

    lax.fori_loop(0, 8, send_back, 0)

    @pl.when(at_home)
    def _():
        ox[slot] = ot[pl.ds(pl.multiple_of(p * 8, 8), 8), :]

    @pl.when(t < TILES - 1)
    def _():
        for copy in strips:
            copy.wait_send()

    for there, copy in sent:

        @pl.when(there)
        def _():
            copy.wait_send()

    @pl.when(at_home)
    def _():
        few = pl.ds(0, PLANES - 1)
        pltpu.make_async_copy(tx.at[few], tx.at[few], in_send).wait()
        pltpu.make_async_copy(ox.at[few], ox.at[few], out_recv).wait()
        pltpu.make_async_copy(ox.at[few], ox.at[few], out_send).wait()

    @pl.when(jnp.logical_not(at_home))
    def _():
        pltpu.make_async_copy(tx, tx, in_send).wait()
        pltpu.make_async_copy(ox, ox, out_recv).wait()
        pltpu.make_async_copy(ox, ox, out_send).wait()


def to_rows(ox, result, res, sem):
    group = lanes_of((8, 128)) // 32
    stores = []
    for ch in range(2):
        for half in range(2):
            for hh in range(2):
                tiles = [ox[ch * 16 + hh * 8 + half * 4 + q] for q in range(4)]
                for y in range(4):
                    line = turn(tiles[0], 32 * (0 - y))
                    for q in range(1, 4):
                        line = jnp.where(group == q, turn(tiles[q], 32 * (q - y)), line)
                    res[pl.ds((ch * 2 + half) * 64 + hh * 32 + y, 8, stride=4), :] = line
            store = pltpu.make_async_copy(
                res.at[pl.ds((ch * 2 + half) * 64, 64), :],
                result.at[ch, 0, :, pl.ds(half * 128, 128)],
                sem.at[ch * 2 + half],
            )
            store.start()
            stores.append(store)
    for store in stores:
        store.wait()


def shards(observed, intersection_strip, axial_taps, lateral_taps, extents, section_skews):
    anywhere = pl.BlockSpec(memory_space=pl.ANY)
    scalars = pl.BlockSpec(memory_space=pltpu.SMEM)
    vmem = pl.BlockSpec(memory_space=pltpu.VMEM)
    rounds = 2 * ITERS
    dma = pltpu.SemaphoreType.DMA
    blocks = pl.pallas_call(
        kernel,
        out_shape=jax.ShapeDtypeStruct((32, 8, 128), F32),
        in_specs=[anywhere, anywhere, scalars, scalars, scalars, scalars],
        out_specs=vmem,
        scratch_shapes=[
            pltpu.VMEM((256, 128), F32),
            pltpu.VMEM((128, 128), F32),
            pltpu.VMEM((128, 128), F32),
            pltpu.VMEM((32, 8, 128), F32),
            pltpu.VMEM((256, 128), F32),
            pltpu.VMEM((rounds, 8, 32, 128), F32),
            pltpu.VMEM((rounds, 8, 8, 128), F32),
            pltpu.VMEM((rounds, 8, 8, 128), F32),
            pltpu.VMEM((rounds, 12, 8, 128), F32),
            pltpu.VMEM((rounds, 12, 8, 128), F32),
            pltpu.VMEM((rounds, 2, 2, 32, 128), F32),
            pltpu.VMEM((2, 12, 32, 128), BF16),
            pltpu.VMEM((2, 12, 32, 128), BF16),
            pltpu.VMEM((1280, 256), BF16),
            pltpu.VMEM((1280, 256), BF16),
            pltpu.VMEM((32, 128), BF16),
            pltpu.VMEM((32, 128), BF16),
            pltpu.VMEM((256, 128), F32),
            dma((4,)),
            dma((4,)),
            dma((4,)),
            dma((4,)),
            dma,
            dma,
            dma((rounds, 8)),
            dma((rounds, 8)),
            dma,
            dma,
        ],
        compiler_params=pltpu.CompilerParams(collective_id=0, has_side_effects=True),
        name="richardson_lucy",
    )(observed, intersection_strip, axial_taps, lateral_taps, extents, section_skews)
    return pl.pallas_call(
        to_rows,
        out_shape=jax.ShapeDtypeStruct(observed.shape, F32),
        in_specs=[vmem],
        out_specs=anywhere,
        scratch_shapes=[pltpu.VMEM((256, 128), F32), dma((4,))],
        name="rows_of_blocks",
    )(blocks)


def solution(mesh):
    in_specs = (
        P(None, "plane", "tile", None),
        P(None, "plane", "tile", None),
        P(),
        P(),
        P("tile"),
        P("tile"),
    )
    out_specs = P(None, "plane", "tile", None)
    return jax.shard_map(shards, mesh=mesh, in_specs=in_specs, out_specs=out_specs, check_vma=False)
```

```python
import jax
import jax.numpy as jnp
from jax import lax
from jax.experimental import pallas as pl
from jax.experimental.pallas import tpu as pltpu
from jax.sharding import PartitionSpec as P

F32 = jnp.float32
BF16 = jnp.bfloat16
MESH = pl.DeviceIdType.MESH
TILES, PLANES, ITERS = 8, 32, 2
KZ, KL = 41, 15


def home_of(chan, row, xt):
    y, turn_x, q = lax.div(row, 4), lax.rem(row, 4), lax.div(xt, 2)
    px = turn_x + lax.rem(y, 2) * (3 - 2 * turn_x)
    return {"tile": 2 * y + lax.rem(xt + q, 2), "plane": 8 * px + 4 * chan + q}


def split(value):
    high = value.astype(BF16)
    return high, (value - high.astype(F32)).astype(BF16)


def lanes_of(shape):
    return lax.broadcasted_iota(jnp.int32, shape, len(shape) - 1)


def turn(value, by):
    by = by % 128
    return value if by == 0 else pltpu.roll(value, by, value.ndim - 1)


def build_lateral(taps, out):
    lane = lanes_of((32, 128))
    row = lax.broadcasted_iota(jnp.int32, (32, 128), 0)
    x_out, y_out = lane % 32, lane // 32
    side, at = row // 8, row % 8
    own_diff = row - x_out + 7
    left = at - 8 - x_out + 7
    right = at + 32 - x_out + 7
    halo_diff = jnp.where(side == 0, left, jnp.where(side == 3, right, -1))
    blocks = []
    for diff in (own_diff, halo_diff):
        block = jnp.zeros((32, 128), F32)
        for j in range(KL):
            block = jnp.where(diff == j, taps[j], block)
        blocks.append(block)
    for d in range(5):
        for y_in in range(4):
            line = jnp.zeros((32, 128), F32)
            for y in range(4):
                k = 4 * (d - 2) + y_in - y + 7
                if 0 <= k < KL:
                    line = jnp.where(y_out == y, taps[k], line)
            for b, block in enumerate(blocks):
                high, low = split(block * line)
                rows = pl.ds(b * 640 + d * 128 + y_in * 32, 32)
                out[rows, 0:128] = high
                out[rows, 128:256] = low


def build_axial(taps, out):
    lane = lanes_of((32, 128))
    row = lax.broadcasted_iota(jnp.int32, (32, 128), 0)
    diff = lane % 32 - row + KZ // 2
    matrix = jnp.zeros((32, 128), F32)
    for j in range(KZ):
        matrix = jnp.where(diff == j, taps[j], matrix)
    high = matrix.astype(BF16).astype(F32)
    both = jnp.where(lane < 64, high, jnp.where(lane < 96, matrix - high, 0.0))
    out[...] = both.astype(BF16)


FAR_FIRST = (4, 3, 5, 2, 6, 1, 7, 0)


def kernel(
    observed, strip, axial, lateral, extents, skews, ox,
    obs_v, strip_s, strip_v, tx, rx, own, sl, sr, hl, hr, yh, eo, eh, wf, wa, zf, za, ot,
    obs_sem, strip_load, strip_send, strip_recv, in_send, in_recv, halo_send, halo_recv, out_send, out_recv,
):
    t = lax.axis_index("tile")
    p = lax.axis_index("plane")
    px, pz = lax.div(p, 8), lax.rem(p, 8)
    y, core = lax.div(t, 2), lax.rem(t, 2)
    c, q_own = lax.div(pz, 4), lax.rem(pz, 4)
    xt = 2 * q_own + lax.rem(core + q_own, 2)
    rr = 4 * y + px + lax.rem(y, 2) * (3 - 2 * px)
    h = lax.rem(rr, 2)
    source = lax.div(rr, 2)
    slot = c * 16 + h * 8 + xt
    at_home = source == t

    def exists(dy, dx):
        fine = (xt + dx >= 0) & (xt + dx < 8)
        return fine & (rr + dy >= 0) & (rr + dy < 2 * TILES)

    around = [(dy, dx) for dy in (-1, 1) for dx in (-1, 1)] + [(0, -1), (0, 1), (-1, 0), (1, 0)]
    after = {"tile": t + 1, "plane": p}
    before = {"tile": t - 1, "plane": p}

    barrier = pltpu.get_barrier_semaphore()

    def greet(to):
        pl.semaphore_signal(barrier, inc=1, device_id=to, device_id_type=MESH)

    for dz in FAR_FIRST:
        for dx in (2, 1, 3, 0):
            to = 8 * lax.rem(px + dx, 4) + lax.rem(pz + dz, 8)
            if dz + dx == 0:

                @pl.when(source != t)
                def _():
                    greet({"tile": source, "plane": to})

            else:
                greet({"tile": source, "plane": to})
    met = PLANES - jnp.where(at_home, 1, 0)
    for dy, dx in around:

        @pl.when(exists(dy, dx))
        def _():
            greet(home_of(c, rr + dy, xt + dx))

        met = met + jnp.where(exists(dy, dx), 1, 0)

    @pl.when(t > 0)
    def _():
        greet(before)

    met = met + jnp.where(t < TILES - 1, 1, 0)

    loads = []
    strip_loads = []
    for ch in range(2):
        for half in range(2):
            i = ch * 2 + half
            lanes = pl.ds(half * 128, 128)
            strip_loads.append(
                pltpu.make_async_copy(strip.at[ch, 0, :, lanes], strip_s.at[pl.ds(i * 32, 32), :], strip_load.at[i])
            )
            loads.append(
                pltpu.make_async_copy(observed.at[ch, 0, :, lanes], obs_v.at[pl.ds(i * 64, 64), :], obs_sem.at[i])
            )
    for load in strip_loads + loads:
        load.start()

    @pl.when(t == 0)
    def _():
        strip_v[...] = jnp.zeros(strip_v.shape, F32)

    for n in range(2 * ITERS):

        @pl.when(xt == 0)
        def _():
            hl[n] = jnp.zeros(hl.shape[1:], F32)

        @pl.when(xt == 7)
        def _():
            hr[n] = jnp.zeros(hr.shape[1:], F32)

        for at, rows, edge_row in ((0, 0, 0), (1, 10, 2 * TILES - 1)):

            @pl.when(rr == edge_row)
            def _():
                yh[n, at] = jnp.zeros(yh.shape[2:], F32)
                hl[n, rows : rows + 2] = jnp.zeros((2,) + hl.shape[2:], F32)
                hr[n, rows : rows + 2] = jnp.zeros((2,) + hr.shape[2:], F32)


    lane = lanes_of((8, 128))
    group = lane // 32

    def to_blocks(hh):
        for ch in range(2):
            for half in range(2):
                base = (ch * 2 + half) * 64 + hh * 32
                rows = [obs_v[pl.ds(base + y, 8, stride=4), :] for y in range(4)]
                for q in range(4):
                    tile = turn(rows[0], 32 * (0 - q))
                    for y in range(1, 4):
                        tile = jnp.where(group == y, turn(rows[y], 32 * (y - q)), tile)
                    tx[ch * 16 + hh * 8 + half * 4 + q] = tile

    def send_blocks(hh):
        for dz in FAR_FIRST:
            zz = lax.rem(pz + dz, 8)
            for cc in range(2):
                xx = 2 * lax.rem(zz, 4) + cc
                to = home_of(lax.div(zz, 4), 2 * t + hh, xx)

                def copy():
                    return pltpu.make_async_remote_copy(
                        src_ref=tx.at[lax.div(zz, 4) * 16 + hh * 8 + xx],
                        dst_ref=rx.at[pl.ds(pl.multiple_of(p * 8, 8), 8), :],
                        send_sem=in_send,
                        recv_sem=in_recv,
                        device_id=to,
                        device_id_type=MESH,
                    )

                if dz == 0:

                    @pl.when((to["plane"] != p) | (to["tile"] != t))
                    def _():
                        copy().start()

                else:
                    copy().start()

    for load in loads + strip_loads:
        load.wait()
    to_blocks(1)
    pl.semaphore_wait(barrier, met)

    strips = []
    for i in range(4):
        rows = pl.ds(i * 32, 32)
        strips.append(
            pltpu.make_async_remote_copy(
                src_ref=strip_s.at[rows, :],
                dst_ref=strip_v.at[rows, :],
                send_sem=strip_send.at[i],
                recv_sem=strip_recv.at[i],
                device_id=after,
                device_id_type=MESH,
            )
        )

    @pl.when(t < TILES - 1)
    def _():
        for copy in strips:
            copy.start()

    send_blocks(1)

    lat = [lateral[c, j] for j in range(KL)]
    ax = [axial[c, j] for j in range(KZ)]
    build_axial(ax, zf)
    build_lateral(lat, wf)
    eo[...] = jnp.zeros(eo.shape, BF16)
    eh[...] = jnp.zeros(eh.shape, BF16)

    @pl.when(t > 0)
    def _():
        for copy in strips:
            copy.wait_recv()

    reach = jnp.where(t == 0, 0, extents[0])
    skew = skews[0]
    shift = skew % 128
    wide_lane = lanes_of((32, 128))
    inside = lax.broadcasted_iota(jnp.int32, (32, 128), 0) < reach
    for ch in range(2):
        low = strip_v[pl.ds(ch * 64, 32), :]
        high = strip_v[pl.ds(ch * 64 + 32, 32), :]
        low = pltpu.roll(low, shift, 1)
        high = pltpu.roll(high, shift, 1)
        wrapped = wide_lane < shift
        first = jnp.where(wrapped, high, low)
        second = jnp.where(wrapped, low, high)
        far = skew >= 128
        for half in range(2):
            moved = jnp.where(far, (second, first)[half], (first, second)[half])
            rows = pl.ds((ch * 2 + half) * 64, 32)
            top = obs_v[rows, :]
            obs_v[rows, :] = jnp.where(inside, 0.5 * (top + moved), top)
    to_blocks(0)
    send_blocks(0)

    @pl.when(at_home)
    def _():
        rx[pl.ds(pl.multiple_of(p * 8, 8), 8), :] = tx[slot]

    build_axial(ax[::-1], za)
    build_lateral(lat[::-1], wa)

    @pl.when(at_home)
    def _():
        most = pl.ds(0, (PLANES - 1) * 8)
        pltpu.make_async_copy(rx.at[most, :], rx.at[most, :], in_recv).wait()

    @pl.when(jnp.logical_not(at_home))
    def _():
        pltpu.make_async_copy(rx, rx, in_recv).wait()

    joined = jnp.concatenate([rx[pl.ds(ys, 32, stride=8), :][None] for ys in range(8)], axis=0)

    edge = (lanes_of((8, 8, 128)) // 8) % 4
    edge2 = (lanes_of((2, 8, 128)) // 8) % 4
    sent = []

    def banded(high, low, w, first, last):
        both = jnp.dot(high, w[first:last, :], preferred_element_type=F32)
        more = jnp.dot(low, w[first:last, 0:128], preferred_element_type=F32)
        return both[:, 0:128] + both[:, 128:256] + more

    def along_z(flat, z):
        n = flat.shape[0] // 32
        high, low = split(flat.reshape(n, 32, 128))
        stacked = jnp.concatenate([high, low, high], axis=1)
        wide = jnp.concatenate([stacked[i] for i in range(n)], axis=1)
        done = jnp.dot(z[:, 0:96], wide, preferred_element_type=F32)
        return [done[:, 128 * i : 128 * i + 128] for i in range(n)]

    def shifted(pad, value, w, base):
        pad[0, 2:10], pad[1, 2:10] = split(value)
        wide = [jnp.concatenate([pad[s, d : d + 8].reshape(256, 128) for d in range(5)], axis=1) for s in range(2)]
        return banded(wide[0], wide[1], w, base, base + 640)

    def unpack(left, right, which):
        sides = [jnp.where(which < 2, turn(left, -8 * k), turn(right, 24 - 8 * k)) for k in range(4)]
        return jnp.concatenate(sides, axis=1)

    def spread(value, w, z, n):
        own[n] = value
        parts = [value[:, 8 * k : 8 * k + 8, :] for k in range(4)]
        to_right = turn(parts[0], -24)
        to_left = parts[0]
        for k in range(1, 4):
            to_right = jnp.where(edge == k, turn(parts[k], 8 * k - 24), to_right)
            to_left = jnp.where(edge == k, turn(parts[k], 8 * k), to_left)
        sr[n] = to_right
        sl[n] = to_left
        copies = {}
        for i, (dy, dx) in enumerate(around):
            rows, size, at = {-1: (0, 2, 10), 0: (0, 8, 2), 1: (6, 2, 0)}[dy]
            if dx == 0:
                src, dst = own.at[n, pl.ds(rows, 2)], yh.at[n, 0 if dy == 1 else 1]
            else:
                src = (sr if dx == 1 else sl).at[n, pl.ds(rows, size)]
                dst = (hl if dx == 1 else hr).at[n, pl.ds(at, size)]
            copy = pltpu.make_async_remote_copy(
                src_ref=src,
                dst_ref=dst,
                send_sem=halo_send.at[n, i],
                recv_sem=halo_recv.at[n, i],
                device_id=home_of(c, rr + dy, xt + dx),
                device_id_type=MESH,
            )
            copies[dy, dx] = copy

            @pl.when(exists(dy, dx))
            def _():
                copy.start()

            sent.append((exists(dy, dx), copy))

        def arrive(dy, dx):
            @pl.when(exists(-dy, -dx))
            def _():
                copies[dy, dx].wait_recv()

        whole = along_z(shifted(eo, value, w, 0), z)
        arrive(0, 1)
        arrive(0, -1)
        beside = unpack(hl[n, 2:10], hr[n, 2:10], edge)
        sides = along_z(shifted(eh, beside, w, 640), z)
        whole = [a + b for a, b in zip(whole, sides)]
        for dy, dx in around:
            if dy != 0:
                arrive(dy, dx)
        ends = []
        for at, rows in ((0, 0), (1, 10)):
            corner = unpack(hl[n, rows : rows + 2], hr[n, rows : rows + 2], edge2)
            ends.append([split(yh[n, at]), split(corner)])
        flat = []
        for at in range(2):
            total = None
            for b in range(2):
                wide = []
                for s in range(2):
                    pair = ends[at][b][s]
                    none = jnp.zeros((32, 128), BF16)
                    if at == 0:
                        lines = ((pair[0], pair[1]), (pair[1], none))
                    else:
                        lines = ((none, pair[0]), (pair[0], pair[1]))
                    wide.append(jnp.concatenate([jnp.concatenate(line, axis=1) for line in lines], axis=0))
                first = b * 640 + (0 if at == 0 else 3 * 128)
                part = banded(wide[0], wide[1], w, first, first + 256)
                total = part if total is None else total + part
            flat.append(total)
        outer = along_z(jnp.concatenate(flat, axis=0), z)
        for i, ys in enumerate((0, 1, 6, 7)):
            whole[ys] = whole[ys] + outer[i]
        return jnp.concatenate([line[None] for line in whole], axis=0)

    estimate = joined
    for sweep in range(ITERS):
        blurred = spread(estimate, wf, zf, 2 * sweep)
        quotient = joined / blurred
        estimate = estimate * spread(quotient, wa, za, 2 * sweep + 1)

    for ys in range(8):
        ot[pl.ds(ys, 32, stride=8), :] = estimate[ys]

    for dz in FAR_FIRST:
        zz = lax.rem(pz + dz, 8)
        for dx in (2, 1, 3, 0):
            to = 8 * lax.rem(px + dx, 4) + zz

            def copy():
                return pltpu.make_async_remote_copy(
                    src_ref=ot.at[pl.ds(pl.multiple_of(to * 8, 8), 8), :],
                    dst_ref=ox.at[slot],
                    send_sem=out_send,
                    recv_sem=out_recv,
                    device_id={"tile": source, "plane": to},
                    device_id_type=MESH,
                )

            if dz + dx == 0:

                @pl.when(jnp.logical_not(at_home))
                def _():
                    copy().start()

            else:
                copy().start()

    @pl.when(at_home)
    def _():
        ox[slot] = ot[pl.ds(pl.multiple_of(p * 8, 8), 8), :]

    @pl.when(t < TILES - 1)
    def _():
        for copy in strips:
            copy.wait_send()

    for there, copy in sent:

        @pl.when(there)
        def _():
            copy.wait_send()

    @pl.when(at_home)
    def _():
        few = pl.ds(0, PLANES - 1)
        pltpu.make_async_copy(tx.at[few], tx.at[few], in_send).wait()
        pltpu.make_async_copy(ox.at[few], ox.at[few], out_recv).wait()
        pltpu.make_async_copy(ox.at[few], ox.at[few], out_send).wait()

    @pl.when(jnp.logical_not(at_home))
    def _():
        pltpu.make_async_copy(tx, tx, in_send).wait()
        pltpu.make_async_copy(ox, ox, out_recv).wait()
        pltpu.make_async_copy(ox, ox, out_send).wait()


def to_rows(ox, result, res, sem):
    group = lanes_of((8, 128)) // 32
    stores = []
    for ch in range(2):
        for half in range(2):
            for hh in range(2):
                tiles = [ox[ch * 16 + hh * 8 + half * 4 + q] for q in range(4)]
                for y in range(4):
                    line = turn(tiles[0], 32 * (0 - y))
                    for q in range(1, 4):
                        line = jnp.where(group == q, turn(tiles[q], 32 * (q - y)), line)
                    res[pl.ds((ch * 2 + half) * 64 + hh * 32 + y, 8, stride=4), :] = line
            store = pltpu.make_async_copy(
                res.at[pl.ds((ch * 2 + half) * 64, 64), :],
                result.at[ch, 0, :, pl.ds(half * 128, 128)],
                sem.at[ch * 2 + half],
            )
            store.start()
            stores.append(store)
    for store in stores:
        store.wait()


def shards(observed, intersection_strip, axial_taps, lateral_taps, extents, section_skews):
    anywhere = pl.BlockSpec(memory_space=pl.ANY)
    scalars = pl.BlockSpec(memory_space=pltpu.SMEM)
    vmem = pl.BlockSpec(memory_space=pltpu.VMEM)
    rounds = 2 * ITERS
    dma = pltpu.SemaphoreType.DMA
    blocks = pl.pallas_call(
        kernel,
        out_shape=pltpu.VMEM((32, 8, 128), F32),
        in_specs=[anywhere, anywhere, scalars, scalars, scalars, scalars],
        out_specs=vmem,
        scratch_shapes=[
            pltpu.VMEM((256, 128), F32),
            pltpu.VMEM((128, 128), F32),
            pltpu.VMEM((128, 128), F32),
            pltpu.VMEM((32, 8, 128), F32),
            pltpu.VMEM((256, 128), F32),
            pltpu.VMEM((rounds, 8, 32, 128), F32),
            pltpu.VMEM((rounds, 8, 8, 128), F32),
            pltpu.VMEM((rounds, 8, 8, 128), F32),
            pltpu.VMEM((rounds, 12, 8, 128), F32),
            pltpu.VMEM((rounds, 12, 8, 128), F32),
            pltpu.VMEM((rounds, 2, 2, 32, 128), F32),
            pltpu.VMEM((2, 12, 32, 128), BF16),
            pltpu.VMEM((2, 12, 32, 128), BF16),
            pltpu.VMEM((1280, 256), BF16),
            pltpu.VMEM((1280, 256), BF16),
            pltpu.VMEM((32, 128), BF16),
            pltpu.VMEM((32, 128), BF16),
            pltpu.VMEM((256, 128), F32),
            dma((4,)),
            dma((4,)),
            dma((4,)),
            dma((4,)),
            dma,
            dma,
            dma((rounds, 8)),
            dma((rounds, 8)),
            dma,
            dma,
        ],
        compiler_params=pltpu.CompilerParams(collective_id=0, has_side_effects=True),
        name="richardson_lucy",
    )(observed, intersection_strip, axial_taps, lateral_taps, extents, section_skews)
    return pl.pallas_call(
        to_rows,
        out_shape=jax.ShapeDtypeStruct(observed.shape, F32),
        in_specs=[vmem],
        out_specs=anywhere,
        scratch_shapes=[pltpu.VMEM((256, 128), F32), dma((4,))],
        name="rows_of_blocks",
    )(pltpu.with_memory_space_constraint(blocks, pltpu.VMEM))


def solution(mesh):
    in_specs = (
        P(None, "plane", "tile", None),
        P(None, "plane", "tile", None),
        P(),
        P(),
        P("tile"),
        P("tile"),
    )
    out_specs = P(None, "plane", "tile", None)
    return jax.shard_map(shards, mesh=mesh, in_specs=in_specs, out_specs=out_specs, check_vma=False)
```

```python
import jax
import jax.numpy as jnp
from jax import lax
from jax.experimental import pallas as pl
from jax.experimental.pallas import tpu as pltpu
from jax.sharding import PartitionSpec as P

F32 = jnp.float32
BF16 = jnp.bfloat16
MESH = pl.DeviceIdType.MESH
TILES, PLANES, ITERS = 8, 32, 2
KZ, KL = 41, 15


def home_of(chan, row, xt):
    y, turn_x, q = lax.div(row, 4), lax.rem(row, 4), lax.div(xt, 2)
    px = turn_x + lax.rem(y, 2) * (3 - 2 * turn_x)
    return {"tile": 2 * y + lax.rem(xt + q, 2), "plane": 8 * px + 4 * chan + q}


def split(value):
    high = value.astype(BF16)
    return high, (value - high.astype(F32)).astype(BF16)


def lanes_of(shape):
    return lax.broadcasted_iota(jnp.int32, shape, len(shape) - 1)


def turn(value, by):
    by = by % 128
    return value if by == 0 else pltpu.roll(value, by, value.ndim - 1)


def build_lateral(taps, out, wide):
    lane = lanes_of((32, 128))
    row = lax.broadcasted_iota(jnp.int32, (32, 128), 0)
    x_lane, y_out = lane % 32, lane // 32
    x_halo = jnp.where(x_lane < 16, x_lane - 16, x_lane + 16)
    row_halo = jnp.where(row < 16, row - 16, row + 16)
    near = (x_lane >= 8) & (x_lane < 24)
    columns = 2 if wide else 1
    blocks = []
    for x_in in (row, row_halo):
        for o in range(columns):
            diff = x_in - (x_halo if o else x_lane) + 7
            if o:
                diff = jnp.where(near, diff, -1)
            block = jnp.zeros((32, 128), F32)
            for j in range(KL):
                block = jnp.where(diff == j, taps[j], block)
            blocks.append(block)
    for d in range(5):
        for y_in in range(4):
            line = jnp.zeros((32, 128), F32)
            for y in range(4):
                k = 4 * (d - 2) + y_in - y + 7
                if 0 <= k < KL:
                    line = jnp.where(y_out == y, taps[k], line)
            for b in range(2):
                rows = pl.ds((b * 640 + d * 128 if wide else d * 256 + b * 128) + y_in * 32, 32)
                for o in range(columns):
                    high, low = split(blocks[b * columns + o] * line)
                    out[rows, o * 128 : o * 128 + 128] = high
                    out[rows, (columns + o) * 128 : (columns + o) * 128 + 128] = low


def build_axial(taps, out):
    lane = lanes_of((32, 128))
    row = lax.broadcasted_iota(jnp.int32, (32, 128), 0)
    diff = lane % 32 - row + KZ // 2
    matrix = jnp.zeros((32, 128), F32)
    for j in range(KZ):
        matrix = jnp.where(diff == j, taps[j], matrix)
    high = matrix.astype(BF16).astype(F32)
    both = jnp.where(lane < 64, high, jnp.where(lane < 96, matrix - high, 0.0))
    out[...] = both.astype(BF16)


FAR_FIRST = (4, 3, 5, 2, 6, 1, 7, 0)


def kernel(
    observed, strip, axial, lateral, extents, skews, ox,
    obs_v, strip_s, strip_v, tx, rx, own, packs, hx, yh, mine, beside, jx, wf, wa, zf, za, ot,
    obs_sem, strip_load, strip_send, strip_recv, in_send, in_recv, halo_send, halo_recv, out_send, out_recv,
):
    t = lax.axis_index("tile")
    p = lax.axis_index("plane")
    px, pz = lax.div(p, 8), lax.rem(p, 8)
    y, core = lax.div(t, 2), lax.rem(t, 2)
    c, q_own = lax.div(pz, 4), lax.rem(pz, 4)
    xt = 2 * q_own + lax.rem(core + q_own, 2)
    rr = 4 * y + px + lax.rem(y, 2) * (3 - 2 * px)
    h = lax.rem(rr, 2)
    source = lax.div(rr, 2)
    slot = c * 16 + h * 8 + xt
    at_home = source == t

    def exists(dy, dx):
        fine = (xt + dx >= 0) & (xt + dx < 8)
        return fine & (rr + dy >= 0) & (rr + dy < 2 * TILES)

    around = [(dy, dx) for dy in (-1, 1) for dx in (-1, 1)] + [(-1, 0), (1, 0), (0, -1), (0, 1)]
    after = {"tile": t + 1, "plane": p}
    before = {"tile": t - 1, "plane": p}

    barrier = pltpu.get_barrier_semaphore()

    def greet(to):
        pl.semaphore_signal(barrier, inc=1, device_id=to, device_id_type=MESH)

    for dz in FAR_FIRST:
        for dx in (2, 1, 3, 0):
            to = 8 * lax.rem(px + dx, 4) + lax.rem(pz + dz, 8)
            if dz + dx == 0:

                @pl.when(source != t)
                def _():
                    greet({"tile": source, "plane": to})

            else:
                greet({"tile": source, "plane": to})
    met = PLANES - jnp.where(at_home, 1, 0)
    for dy, dx in around:

        @pl.when(exists(dy, dx))
        def _():
            greet(home_of(c, rr + dy, xt + dx))

        met = met + jnp.where(exists(dy, dx), 1, 0)

    @pl.when(t > 0)
    def _():
        greet(before)

    met = met + jnp.where(t < TILES - 1, 1, 0)

    loads = []
    strip_loads = []
    for ch in range(2):
        for half in range(2):
            i = ch * 2 + half
            lanes = pl.ds(half * 128, 128)
            strip_loads.append(
                pltpu.make_async_copy(strip.at[ch, 0, :, lanes], strip_s.at[pl.ds(i * 32, 32), :], strip_load.at[i])
            )
            loads.append(
                pltpu.make_async_copy(observed.at[ch, 0, :, lanes], obs_v.at[pl.ds(i * 64, 64), :], obs_sem.at[i])
            )
    for load in strip_loads + loads:
        load.start()

    @pl.when(t == 0)
    def _():
        strip_v[...] = jnp.zeros(strip_v.shape, F32)

    for n in range(ITERS):

        @pl.when(xt == 0)
        def _():
            hx[n, 0:2] = jnp.zeros((2,) + hx.shape[2:], F32)

        @pl.when(xt == 7)
        def _():
            hx[n, 2:4] = jnp.zeros((2,) + hx.shape[2:], F32)

        for at, rows, edge_row in ((0, 0, 0), (1, 12, 2 * TILES - 1)):

            @pl.when(rr == edge_row)
            def _():
                yh[n, at] = jnp.zeros(yh.shape[2:], F32)
                hx[n, :, rows : rows + 4] = jnp.zeros((4, 4) + hx.shape[3:], F32)

    lane = lanes_of((8, 128))
    group = lane // 32

    def to_blocks(hh):
        for ch in range(2):
            for half in range(2):
                base = (ch * 2 + half) * 64 + hh * 32
                rows = [obs_v[pl.ds(base + y, 8, stride=4), :] for y in range(4)]
                for q in range(4):
                    tile = turn(rows[0], 32 * (0 - q))
                    for y in range(1, 4):
                        tile = jnp.where(group == y, turn(rows[y], 32 * (y - q)), tile)
                    tx[ch * 16 + hh * 8 + half * 4 + q] = tile

    def send_blocks(hh):
        for dz in FAR_FIRST:
            zz = lax.rem(pz + dz, 8)
            for cc in range(2):
                xx = 2 * lax.rem(zz, 4) + cc
                to = home_of(lax.div(zz, 4), 2 * t + hh, xx)

                def copy():
                    return pltpu.make_async_remote_copy(
                        src_ref=tx.at[lax.div(zz, 4) * 16 + hh * 8 + xx],
                        dst_ref=rx.at[pl.ds(pl.multiple_of(p * 8, 8), 8), :],
                        send_sem=in_send,
                        recv_sem=in_recv,
                        device_id=to,
                        device_id_type=MESH,
                    )

                if dz == 0:

                    @pl.when((to["plane"] != p) | (to["tile"] != t))
                    def _():
                        copy().start()

                else:
                    copy().start()

    for load in loads + strip_loads:
        load.wait()
    to_blocks(1)
    pl.semaphore_wait(barrier, met)

    strips = []
    for i in range(4):
        rows = pl.ds(i * 32, 32)
        strips.append(
            pltpu.make_async_remote_copy(
                src_ref=strip_s.at[rows, :],
                dst_ref=strip_v.at[rows, :],
                send_sem=strip_send.at[i],
                recv_sem=strip_recv.at[i],
                device_id=after,
                device_id_type=MESH,
            )
        )

    @pl.when(t < TILES - 1)
    def _():
        for copy in strips:
            copy.start()

    send_blocks(1)

    @pl.when(t > 0)
    def _():
        for copy in strips:
            copy.wait_recv()

    reach = jnp.where(t == 0, 0, extents[0])
    skew = skews[0]
    shift = skew % 128
    wide_lane = lanes_of((32, 128))
    inside = lax.broadcasted_iota(jnp.int32, (32, 128), 0) < reach
    for ch in range(2):
        low = strip_v[pl.ds(ch * 64, 32), :]
        high = strip_v[pl.ds(ch * 64 + 32, 32), :]
        low = pltpu.roll(low, shift, 1)
        high = pltpu.roll(high, shift, 1)
        wrapped = wide_lane < shift
        first = jnp.where(wrapped, high, low)
        second = jnp.where(wrapped, low, high)
        far = skew >= 128
        for half in range(2):
            moved = jnp.where(far, (second, first)[half], (first, second)[half])
            rows = pl.ds((ch * 2 + half) * 64, 32)
            top = obs_v[rows, :]
            obs_v[rows, :] = jnp.where(inside, 0.5 * (top + moved), top)
    to_blocks(0)
    send_blocks(0)

    @pl.when(at_home)
    def _():
        rx[pl.ds(pl.multiple_of(p * 8, 8), 8), :] = tx[slot]

    lat = [lateral[c, j] for j in range(KL)]
    ax = [axial[c, j] for j in range(KZ)]
    build_axial(ax, zf)
    build_lateral(lat, wf, True)
    mine[...] = jnp.zeros(mine.shape, BF16)
    beside[...] = jnp.zeros(beside.shape, BF16)
    build_axial(ax[::-1], za)
    build_lateral(lat[::-1], wa, False)

    @pl.when(at_home)
    def _():
        most = pl.ds(0, (PLANES - 1) * 8)
        pltpu.make_async_copy(rx.at[most, :], rx.at[most, :], in_recv).wait()

    @pl.when(jnp.logical_not(at_home))
    def _():
        pltpu.make_async_copy(rx, rx, in_recv).wait()

    joined = jnp.concatenate([rx[pl.ds(ys, 32, stride=8), :][None] for ys in range(8)], axis=0)

    sent = []

    def regroup(lines):
        group = (lanes_of(lines[0].shape) // 8) % 4
        done = []
        for g in range(4):
            total = turn(lines[0], 8 * (0 - g))
            for k in range(1, 4):
                total = jnp.where(group == k, turn(lines[k], 8 * (k - g)), total)
            done.append(total)
        return done

    def banded(high, low, w, first):
        columns, rows = w.shape[1] // 2, pl.ds(first, high.shape[1])
        both = jnp.dot(high, w[rows, :], preferred_element_type=F32)
        more = jnp.dot(low, w[rows, 0:columns], preferred_element_type=F32)
        return both[:, 0:columns] + both[:, columns:] + more

    def along_z(flat, z):
        n, columns = flat.shape[0] // 32, flat.shape[1]
        high, low = split(flat.reshape(n, 32, columns))
        stacked = jnp.concatenate([high, low, high], axis=1)
        wide = jnp.concatenate([stacked[i] for i in range(n)], axis=1)
        done = jnp.dot(z[:, 0:96], wide, preferred_element_type=F32)
        return [done[:, columns * i : columns * (i + 1)] for i in range(n)]

    def padded(pad, value, first):
        pad[0, 4:12], pad[1, 4:12] = split(value)
        wide = [jnp.concatenate([pad[i, d : d + 12].reshape(384, 128) for d in range(5)], axis=1) for i in range(2)]
        return banded(wide[0], wide[1], wf, first)

    def beyond(value, at, first):
        wide = []
        for part in split(value):
            none = jnp.zeros((32, 128), BF16)
            columns = []
            for d in range(4):
                lines = [i + d if at == 0 else i + d - 3 for i in range(4)]
                columns.append(jnp.concatenate([part[i] if 0 <= i < 4 else none for i in lines], axis=0))
            wide.append(jnp.concatenate(columns, axis=1))
        return banded(wide[0], wide[1], wf, first + 128 * at)

    def forward(value, n):
        own[n] = value
        for g, pack in enumerate(regroup([value[:, 8 * k : 8 * k + 8, :] for k in range(4)])):
            packs[n, g] = pack
        copies = {}
        for i, (dy, dx) in enumerate(around):
            rows, size, at = {-1: (0, 4, 12), 0: (0, 8, 4), 1: (4, 4, 0)}[dy]
            if dx == 0:
                src, dst = own.at[n, pl.ds(rows, 4)], yh.at[n, 0 if dy == 1 else 1]
            else:
                side = (2, 0) if dx == 1 else (0, 2)
                src = packs.at[n, pl.ds(side[0], 2), pl.ds(rows, size)]
                dst = hx.at[n, pl.ds(side[1], 2), pl.ds(at, size)]
            copy = pltpu.make_async_remote_copy(
                src_ref=src,
                dst_ref=dst,
                send_sem=halo_send.at[n, i],
                recv_sem=halo_recv.at[n, i],
                device_id=home_of(c, rr + dy, xt + dx),
                device_id_type=MESH,
            )
            copies[dy, dx] = copy

            @pl.when(exists(dy, dx))
            def _():
                copy.start()

            sent.append((exists(dy, dx), copy))
        def arrive(which):
            for dy, dx in around:
                if which(dy):

                    @pl.when(exists(-dy, -dx))
                    def _():
                        copies[dy, dx].wait_recv()

        inner = padded(mine, value, 0)
        arrive(lambda dy: dy == 0)
        sides = jnp.concatenate(regroup([hx[n, g, 4:12] for g in range(4)]), axis=1)
        blurred = along_z(inner + padded(beside, sides, 640), zf)
        arrive(lambda dy: dy != 0)
        outer = []
        for at, rows in ((0, 0), (1, 12)):
            corners = jnp.concatenate(regroup([hx[n, g, rows : rows + 4] for g in range(4)]), axis=1)
            outer.append(beyond(yh[n, at], at, 0) + beyond(corners, at, 640))
            if n == 0:
                edge, near = ((0, 2), (2, 4)) if at == 0 else ((10, 12), (0, 2))
                jx[edge[0] : edge[1], :, 0:128] = yh[n, at, near[0] : near[1]]
                jx[edge[0] : edge[1], :, 128:256] = corners[near[0] : near[1]]
        if n == 0:
            jx[2:10, :, 0:128] = value
            jx[2:10, :, 128:256] = sides
        outer = along_z(jnp.concatenate(outer, axis=0), zf)
        for i in range(8):
            o = i if i < 4 else i + 4
            blurred[o] = blurred[o] + outer[i]
        return blurred

    def shifts(lines, size):
        return jnp.concatenate([lines[d : d + size].reshape(size * 32, 256) for d in range(5)], axis=1)

    wide_lane = lanes_of((32, 256))
    near = (wide_lane // 8) % 4
    on_slab = (wide_lane < 128) | ((near == 1) & (xt > 0)) | ((near == 2) & (xt < 7))
    estimate = joined
    for sweep in range(ITERS):
        blurred = forward(estimate, sweep)
        quotient = []
        for i in range(12):
            inside = on_slab
            if i < 2:
                inside = inside & (rr > 0)
            if i >= 10:
                inside = inside & (rr < 2 * TILES - 1)
            quotient.append(jnp.where(inside, jx[i] / blurred[i], 0.0)[None])
        high, low = split(jnp.concatenate(quotient, axis=0))
        factor = along_z(banded(shifts(high, 8), shifts(low, 8), wa, 0), za)
        estimate = estimate * jnp.concatenate([line[None] for line in factor], axis=0)

    for ys in range(8):
        ot[pl.ds(ys, 32, stride=8), :] = estimate[ys]

    for dz in FAR_FIRST:
        zz = lax.rem(pz + dz, 8)
        for dx in (2, 1, 3, 0):
            to = 8 * lax.rem(px + dx, 4) + zz

            def copy():
                return pltpu.make_async_remote_copy(
                    src_ref=ot.at[pl.ds(pl.multiple_of(to * 8, 8), 8), :],
                    dst_ref=ox.at[slot],
                    send_sem=out_send,
                    recv_sem=out_recv,
                    device_id={"tile": source, "plane": to},
                    device_id_type=MESH,
                )

            if dz + dx == 0:

                @pl.when(jnp.logical_not(at_home))
                def _():
                    copy().start()

            else:
                copy().start()

    @pl.when(at_home)
    def _():
        ox[slot] = ot[pl.ds(pl.multiple_of(p * 8, 8), 8), :]

    @pl.when(t < TILES - 1)
    def _():
        for copy in strips:
            copy.wait_send()

    for there, copy in sent:

        @pl.when(there)
        def _():
            copy.wait_send()

    @pl.when(at_home)
    def _():
        few = pl.ds(0, PLANES - 1)
        pltpu.make_async_copy(tx.at[few], tx.at[few], in_send).wait()
        pltpu.make_async_copy(ox.at[few], ox.at[few], out_recv).wait()
        pltpu.make_async_copy(ox.at[few], ox.at[few], out_send).wait()

    @pl.when(jnp.logical_not(at_home))
    def _():
        pltpu.make_async_copy(tx, tx, in_send).wait()
        pltpu.make_async_copy(ox, ox, out_recv).wait()
        pltpu.make_async_copy(ox, ox, out_send).wait()


def to_rows(ox, result, res, sem):
    group = lanes_of((8, 128)) // 32
    stores = []
    for ch in range(2):
        for half in range(2):
            for hh in range(2):
                tiles = [ox[ch * 16 + hh * 8 + half * 4 + q] for q in range(4)]
                for y in range(4):
                    line = turn(tiles[0], 32 * (0 - y))
                    for q in range(1, 4):
                        line = jnp.where(group == q, turn(tiles[q], 32 * (q - y)), line)
                    res[pl.ds((ch * 2 + half) * 64 + hh * 32 + y, 8, stride=4), :] = line
            store = pltpu.make_async_copy(
                res.at[pl.ds((ch * 2 + half) * 64, 64), :],
                result.at[ch, 0, :, pl.ds(half * 128, 128)],
                sem.at[ch * 2 + half],
            )
            store.start()
            stores.append(store)
    for store in stores:
        store.wait()


def shards(observed, intersection_strip, axial_taps, lateral_taps, extents, section_skews):
    anywhere = pl.BlockSpec(memory_space=pl.ANY)
    scalars = pl.BlockSpec(memory_space=pltpu.SMEM)
    vmem = pl.BlockSpec(memory_space=pltpu.VMEM)
    dma = pltpu.SemaphoreType.DMA
    blocks = pl.pallas_call(
        kernel,
        out_shape=pltpu.VMEM((32, 8, 128), F32),
        in_specs=[anywhere, anywhere, scalars, scalars, scalars, scalars],
        out_specs=vmem,
        scratch_shapes=[
            pltpu.VMEM((256, 128), F32),
            pltpu.VMEM((128, 128), F32),
            pltpu.VMEM((128, 128), F32),
            pltpu.VMEM((32, 8, 128), F32),
            pltpu.VMEM((256, 128), F32),
            pltpu.VMEM((ITERS, 8, 32, 128), F32),
            pltpu.VMEM((ITERS, 4, 8, 8, 128), F32),
            pltpu.VMEM((ITERS, 4, 16, 8, 128), F32),
            pltpu.VMEM((ITERS, 2, 4, 32, 128), F32),
            pltpu.VMEM((2, 16, 32, 128), BF16),
            pltpu.VMEM((2, 16, 32, 128), BF16),
            pltpu.VMEM((12, 32, 256), F32),
            pltpu.VMEM((1280, 512), BF16),
            pltpu.VMEM((1280, 256), BF16),
            pltpu.VMEM((32, 128), BF16),
            pltpu.VMEM((32, 128), BF16),
            pltpu.VMEM((256, 128), F32),
            dma((4,)),
            dma((4,)),
            dma((4,)),
            dma((4,)),
            dma,
            dma,
            dma((ITERS, 8)),
            dma((ITERS, 8)),
            dma,
            dma,
        ],
        compiler_params=pltpu.CompilerParams(collective_id=0, has_side_effects=True),
        name="richardson_lucy",
    )(observed, intersection_strip, axial_taps, lateral_taps, extents, section_skews)
    return pl.pallas_call(
        to_rows,
        out_shape=jax.ShapeDtypeStruct(observed.shape, F32),
        in_specs=[vmem],
        out_specs=anywhere,
        scratch_shapes=[pltpu.VMEM((256, 128), F32), dma((4,))],
        name="rows_of_blocks",
    )(pltpu.with_memory_space_constraint(blocks, pltpu.VMEM))


def solution(mesh):
    in_specs = (
        P(None, "plane", "tile", None),
        P(None, "plane", "tile", None),
        P(),
        P(),
        P("tile"),
        P("tile"),
    )
    out_specs = P(None, "plane", "tile", None)
    return jax.shard_map(shards, mesh=mesh, in_specs=in_specs, out_specs=out_specs, check_vma=False)
```

```python
import jax
import jax.numpy as jnp
from jax import lax
from jax.experimental import pallas as pl
from jax.experimental.pallas import tpu as pltpu
from jax.sharding import PartitionSpec as P

F32 = jnp.float32
BF16 = jnp.bfloat16
MESH = pl.DeviceIdType.MESH
TILES, PLANES, ITERS = 8, 32, 2
KZ, KL = 41, 15


def home_of(chan, row, xt):
    y, turn_x, q = lax.div(row, 4), lax.rem(row, 4), lax.div(xt, 2)
    px = turn_x + lax.rem(y, 2) * (3 - 2 * turn_x)
    return {"tile": 2 * y + lax.rem(xt + q, 2), "plane": 8 * px + 4 * chan + q}


def split(value):
    high = value.astype(BF16)
    return high, (value - high.astype(F32)).astype(BF16)


def lanes_of(shape):
    return lax.broadcasted_iota(jnp.int32, shape, len(shape) - 1)


def turn(value, by):
    by = by % 128
    return value if by == 0 else pltpu.roll(value, by, value.ndim - 1)


def build_lateral(taps, out, wide):
    lane = lanes_of((32, 128))
    row = lax.broadcasted_iota(jnp.int32, (32, 128), 0)
    x_lane, y_out = lane % 32, lane // 32
    x_halo = jnp.where(x_lane < 16, x_lane - 16, x_lane + 16)
    row_halo = jnp.where(row < 16, row - 16, row + 16)
    near = (x_lane >= 8) & (x_lane < 24)
    columns = 2 if wide else 1
    blocks = []
    for x_in in (row, row_halo):
        for o in range(columns):
            diff = x_in - (x_halo if o else x_lane) + 7
            if o:
                diff = jnp.where(near, diff, -1)
            block = jnp.zeros((32, 128), F32)
            for j in range(KL):
                block = jnp.where(diff == j, taps[j], block)
            blocks.append(block)
    for d in range(5):
        for y_in in range(4):
            line = jnp.zeros((32, 128), F32)
            for y in range(4):
                k = 4 * (d - 2) + y_in - y + 7
                if 0 <= k < KL:
                    line = jnp.where(y_out == y, taps[k], line)
            for b in range(2):
                rows = pl.ds((b * 640 + d * 128 if wide else d * 256 + b * 128) + y_in * 32, 32)
                for o in range(columns):
                    high, low = split(blocks[b * columns + o] * line)
                    out[rows, o * 128 : o * 128 + 128] = high
                    out[rows, (columns + o) * 128 : (columns + o) * 128 + 128] = low


def build_axial(taps, out):
    lane = lanes_of((32, 128))
    row = lax.broadcasted_iota(jnp.int32, (32, 128), 0)
    diff = lane % 32 - row + KZ // 2
    matrix = jnp.zeros((32, 128), F32)
    for j in range(KZ):
        matrix = jnp.where(diff == j, taps[j], matrix)
    high = matrix.astype(BF16).astype(F32)
    both = jnp.where(lane < 64, high, jnp.where(lane < 96, matrix - high, 0.0))
    out[...] = both.astype(BF16)


FAR_FIRST = (4, 3, 5, 2, 6, 1, 7, 0)


def kernel(
    observed, strip, axial_in, lateral_in, extents_in, skews_in, ox,
    axial, lateral, extents, skews, small_sem,
    obs_v, strip_s, strip_v, tx, rx, own, packs, hx, yh, mine, beside, qh, ql, jx, wf, wa, zf, za, ot,
    obs_sem, strip_load, strip_send, strip_recv, in_send, in_recv, halo_send, halo_recv, out_send, out_recv,
):
    t = lax.axis_index("tile")
    p = lax.axis_index("plane")
    px, pz = lax.div(p, 8), lax.rem(p, 8)
    y, core = lax.div(t, 2), lax.rem(t, 2)
    c, q_own = lax.div(pz, 4), lax.rem(pz, 4)
    xt = 2 * q_own + lax.rem(core + q_own, 2)
    rr = 4 * y + px + lax.rem(y, 2) * (3 - 2 * px)
    h = lax.rem(rr, 2)
    source = lax.div(rr, 2)
    slot = c * 16 + h * 8 + xt
    at_home = source == t

    def exists(dy, dx):
        fine = (xt + dx >= 0) & (xt + dx < 8)
        return fine & (rr + dy >= 0) & (rr + dy < 2 * TILES)

    around = [(0, -1), (0, 1)] + [(dy, dx) for dy in (-1, 1) for dx in (-1, 1)] + [(-1, 0), (1, 0)]
    after = {"tile": t + 1, "plane": p}
    before = {"tile": t - 1, "plane": p}

    barrier = pltpu.get_barrier_semaphore()

    def greet(to):
        pl.semaphore_signal(barrier, inc=1, device_id=to, device_id_type=MESH)

    for dz in FAR_FIRST:
        for dx in (2, 1, 3, 0):
            to = 8 * lax.rem(px + dx, 4) + lax.rem(pz + dz, 8)
            if dz + dx == 0:

                @pl.when(source != t)
                def _():
                    greet({"tile": source, "plane": to})

            else:
                greet({"tile": source, "plane": to})
    met = PLANES - jnp.where(at_home, 1, 0)
    for dy, dx in around:

        @pl.when(exists(dy, dx))
        def _():
            greet(home_of(c, rr + dy, xt + dx))

        met = met + jnp.where(exists(dy, dx), 1, 0)

    @pl.when(t > 0)
    def _():
        greet(before)

    met = met + jnp.where(t < TILES - 1, 1, 0)

    loads = []
    strip_loads = []
    for ch in range(2):
        for half in range(2):
            i = ch * 2 + half
            lanes = pl.ds(half * 128, 128)
            strip_loads.append(
                pltpu.make_async_copy(strip.at[ch, 0, :, lanes], strip_s.at[pl.ds(i * 32, 32), :], strip_load.at[i])
            )
            loads.append(
                pltpu.make_async_copy(observed.at[ch, 0, :, lanes], obs_v.at[pl.ds(i * 64, 64), :], obs_sem.at[i])
            )
    scalar_loads = []
    for i, (src, dst) in enumerate(((axial_in, axial), (lateral_in, lateral), (extents_in, extents), (skews_in, skews))):
        scalar_loads.append(pltpu.make_async_copy(src, dst, small_sem.at[i]))
    for load in strip_loads + loads + scalar_loads:
        load.start()

    @pl.when(t == 0)
    def _():
        strip_v[...] = jnp.zeros(strip_v.shape, F32)

    for n in range(ITERS):

        @pl.when(xt == 0)
        def _():
            hx[n, 0:2] = jnp.zeros((2,) + hx.shape[2:], F32)

        @pl.when(xt == 7)
        def _():
            hx[n, 2:4] = jnp.zeros((2,) + hx.shape[2:], F32)

        for at, rows, edge_row in ((0, 0, 0), (1, 12, 2 * TILES - 1)):

            @pl.when(rr == edge_row)
            def _():
                yh[n, at] = jnp.zeros(yh.shape[2:], F32)
                hx[n, :, rows : rows + 4] = jnp.zeros((4, 4) + hx.shape[3:], F32)

    lane = lanes_of((8, 128))
    group = lane // 32

    def to_blocks(hh):
        for ch in range(2):
            for half in range(2):
                base = (ch * 2 + half) * 64 + hh * 32
                rows = [obs_v[pl.ds(base + y, 8, stride=4), :] for y in range(4)]
                for q in range(4):
                    tile = turn(rows[0], 32 * (0 - q))
                    for y in range(1, 4):
                        tile = jnp.where(group == y, turn(rows[y], 32 * (y - q)), tile)
                    tx[ch * 16 + hh * 8 + half * 4 + q] = tile

    def send_blocks(hh):
        for dz in FAR_FIRST:
            zz = lax.rem(pz + dz, 8)
            for cc in range(2):
                xx = 2 * lax.rem(zz, 4) + cc
                to = home_of(lax.div(zz, 4), 2 * t + hh, xx)

                def copy():
                    return pltpu.make_async_remote_copy(
                        src_ref=tx.at[lax.div(zz, 4) * 16 + hh * 8 + xx],
                        dst_ref=rx.at[pl.ds(pl.multiple_of(p * 8, 8), 8), :],
                        send_sem=in_send,
                        recv_sem=in_recv,
                        device_id=to,
                        device_id_type=MESH,
                    )

                if dz == 0:

                    @pl.when((to["plane"] != p) | (to["tile"] != t))
                    def _():
                        copy().start()

                else:
                    copy().start()

    for load in loads + strip_loads + scalar_loads:
        load.wait()
    to_blocks(1)
    pl.semaphore_wait(barrier, met)

    strips = []
    for i in range(4):
        rows = pl.ds(i * 32, 32)
        strips.append(
            pltpu.make_async_remote_copy(
                src_ref=strip_s.at[rows, :],
                dst_ref=strip_v.at[rows, :],
                send_sem=strip_send.at[i],
                recv_sem=strip_recv.at[i],
                device_id=after,
                device_id_type=MESH,
            )
        )

    @pl.when(t < TILES - 1)
    def _():
        for copy in strips:
            copy.start()

    send_blocks(1)

    @pl.when(t > 0)
    def _():
        for copy in strips:
            copy.wait_recv()

    reach = jnp.where(t == 0, 0, extents[0])
    skew = skews[0]
    shift = skew % 128
    wide_lane = lanes_of((32, 128))
    inside = lax.broadcasted_iota(jnp.int32, (32, 128), 0) < reach
    for ch in range(2):
        low = strip_v[pl.ds(ch * 64, 32), :]
        high = strip_v[pl.ds(ch * 64 + 32, 32), :]
        low = pltpu.roll(low, shift, 1)
        high = pltpu.roll(high, shift, 1)
        wrapped = wide_lane < shift
        first = jnp.where(wrapped, high, low)
        second = jnp.where(wrapped, low, high)
        far = skew >= 128
        for half in range(2):
            moved = jnp.where(far, (second, first)[half], (first, second)[half])
            rows = pl.ds((ch * 2 + half) * 64, 32)
            top = obs_v[rows, :]
            obs_v[rows, :] = jnp.where(inside, 0.5 * (top + moved), top)
    to_blocks(0)
    send_blocks(0)

    @pl.when(at_home)
    def _():
        rx[pl.ds(pl.multiple_of(p * 8, 8), 8), :] = tx[slot]

    lat = [lateral[c, j] for j in range(KL)]
    ax = [axial[c, j] for j in range(KZ)]
    build_axial(ax, zf)
    build_lateral(lat, wf, True)
    mine[...] = jnp.zeros(mine.shape, BF16)
    beside[...] = jnp.zeros(beside.shape, BF16)
    build_axial(ax[::-1], za)
    build_lateral(lat[::-1], wa, False)

    @pl.when(at_home)
    def _():
        most = pl.ds(0, (PLANES - 1) * 8)
        pltpu.make_async_copy(rx.at[most, :], rx.at[most, :], in_recv).wait()

    @pl.when(jnp.logical_not(at_home))
    def _():
        pltpu.make_async_copy(rx, rx, in_recv).wait()

    joined = jnp.concatenate([rx[pl.ds(ys, 32, stride=8), :][None] for ys in range(8)], axis=0)

    sent = []

    def regroup(lines):
        group = (lanes_of(lines[0].shape) // 8) % 4
        done = []
        for g in range(4):
            total = turn(lines[0], 8 * (0 - g))
            for k in range(1, 4):
                total = jnp.where(group == k, turn(lines[k], 8 * (k - g)), total)
            done.append(total)
        return done

    def banded(high, low, w, first):
        columns, rows = w.shape[1] // 2, pl.ds(first, high.shape[1])
        both = jnp.dot(high, w[rows, :], preferred_element_type=F32)
        more = jnp.dot(low, w[rows, 0:columns], preferred_element_type=F32)
        return both[:, 0:columns] + both[:, columns:] + more

    def along_z(flat, z):
        n, columns = flat.shape[0] // 32, flat.shape[1]
        high, low = split(flat.reshape(n, 32, columns))
        stacked = jnp.concatenate([high, low, high], axis=1)
        wide = jnp.concatenate([stacked[i] for i in range(n)], axis=1)
        done = jnp.dot(z[:, 0:96], wide, preferred_element_type=F32)
        return [done[:, columns * i : columns * (i + 1)] for i in range(n)]

    def padded(pad, value, first):
        pad[0, 4:12], pad[1, 4:12] = split(value)
        wide = [jnp.concatenate([pad[i, d : d + 12].reshape(384, 128) for d in range(5)], axis=1) for i in range(2)]
        return banded(wide[0], wide[1], wf, first)

    def beyond(value, at, first):
        wide = []
        for part in split(value):
            none = jnp.zeros((32, 128), BF16)
            columns = []
            for d in range(4):
                lines = [i + d if at == 0 else i + d - 3 for i in range(4)]
                columns.append(jnp.concatenate([part[i] if 0 <= i < 4 else none for i in lines], axis=0))
            wide.append(jnp.concatenate(columns, axis=1))
        return banded(wide[0], wide[1], wf, first + 128 * at)

    def forward(value, n):
        own[n] = value
        for g, pack in enumerate(regroup([value[:, 8 * k : 8 * k + 8, :] for k in range(4)])):
            packs[n, g] = pack
        copies = {}
        for i, (dy, dx) in enumerate(around):
            rows, size, at = {-1: (0, 4, 12), 0: (0, 8, 4), 1: (4, 4, 0)}[dy]
            if dx == 0:
                src, dst = own.at[n, pl.ds(rows, 4)], yh.at[n, 0 if dy == 1 else 1]
            else:
                side = (2, 0) if dx == 1 else (0, 2)
                src = packs.at[n, pl.ds(side[0], 2), pl.ds(rows, size)]
                dst = hx.at[n, pl.ds(side[1], 2), pl.ds(at, size)]
            copy = pltpu.make_async_remote_copy(
                src_ref=src,
                dst_ref=dst,
                send_sem=halo_send.at[n, i],
                recv_sem=halo_recv.at[n, i],
                device_id=home_of(c, rr + dy, xt + dx),
                device_id_type=MESH,
            )
            copies[dy, dx] = copy

            @pl.when(exists(dy, dx))
            def _():
                copy.start()

            sent.append((exists(dy, dx), copy))
        def arrive(which):
            for dy, dx in around:
                if which(dy):

                    @pl.when(exists(-dy, -dx))
                    def _():
                        copies[dy, dx].wait_recv()

        inner = padded(mine, value, 0)
        arrive(lambda dy: dy == 0)
        sides = jnp.concatenate(regroup([hx[n, g, 4:12] for g in range(4)]), axis=1)
        blurred = along_z(inner + padded(beside, sides, 640), zf)
        arrive(lambda dy: dy != 0)
        outer = []
        for at, rows in ((0, 0), (1, 12)):
            corners = jnp.concatenate(regroup([hx[n, g, rows : rows + 4] for g in range(4)]), axis=1)
            outer.append(beyond(yh[n, at], at, 0) + beyond(corners, at, 640))
            if n == 0:
                edge, near = ((0, 2), (2, 4)) if at == 0 else ((10, 12), (0, 2))
                jx[edge[0] : edge[1], :, 0:128] = yh[n, at, near[0] : near[1]]
                jx[edge[0] : edge[1], :, 128:256] = corners[near[0] : near[1]]
        if n == 0:
            jx[2:10, :, 0:128] = value
            jx[2:10, :, 128:256] = sides
        outer = along_z(jnp.concatenate(outer, axis=0), zf)
        for i in range(8):
            o = i if i < 4 else i + 4
            blurred[o] = blurred[o] + outer[i]
        return blurred

    def shifts(lines, size):
        return jnp.concatenate([lines[d : d + size].reshape(size * 32, 256) for d in range(5)], axis=1)

    wide_lane = lanes_of((32, 256))
    near = (wide_lane // 8) % 4
    on_slab = (wide_lane < 128) | ((near == 1) & (xt > 0)) | ((near == 2) & (xt < 7))
    estimate = joined
    for sweep in range(ITERS):
        blurred = forward(estimate, sweep)
        for i in range(12):
            inside = on_slab
            if i < 2:
                inside = inside & (rr > 0)
            if i >= 10:
                inside = inside & (rr < 2 * TILES - 1)
            qh[i], ql[i] = split(jnp.where(inside, jx[i] / blurred[i], 0.0))
        factor = along_z(banded(shifts(qh, 8), shifts(ql, 8), wa, 0), za)
        estimate = estimate * jnp.concatenate([line[None] for line in factor], axis=0)

    for ys in range(8):
        ot[pl.ds(ys, 32, stride=8), :] = estimate[ys]

    for dz in FAR_FIRST:
        zz = lax.rem(pz + dz, 8)
        for dx in (2, 1, 3, 0):
            to = 8 * lax.rem(px + dx, 4) + zz

            def copy():
                return pltpu.make_async_remote_copy(
                    src_ref=ot.at[pl.ds(pl.multiple_of(to * 8, 8), 8), :],
                    dst_ref=ox.at[slot],
                    send_sem=out_send,
                    recv_sem=out_recv,
                    device_id={"tile": source, "plane": to},
                    device_id_type=MESH,
                )

            if dz + dx == 0:

                @pl.when(jnp.logical_not(at_home))
                def _():
                    copy().start()

            else:
                copy().start()

    @pl.when(at_home)
    def _():
        ox[slot] = ot[pl.ds(pl.multiple_of(p * 8, 8), 8), :]

    @pl.when(t < TILES - 1)
    def _():
        for copy in strips:
            copy.wait_send()

    for there, copy in sent:

        @pl.when(there)
        def _():
            copy.wait_send()

    @pl.when(at_home)
    def _():
        few = pl.ds(0, PLANES - 1)
        pltpu.make_async_copy(tx.at[few], tx.at[few], in_send).wait()
        pltpu.make_async_copy(ox.at[few], ox.at[few], out_recv).wait()
        pltpu.make_async_copy(ox.at[few], ox.at[few], out_send).wait()

    @pl.when(jnp.logical_not(at_home))
    def _():
        pltpu.make_async_copy(tx, tx, in_send).wait()
        pltpu.make_async_copy(ox, ox, out_recv).wait()
        pltpu.make_async_copy(ox, ox, out_send).wait()


def to_rows(ox, result, res, sem):
    group = lanes_of((8, 128)) // 32
    stores = []
    for ch in range(2):
        for half in range(2):
            for hh in range(2):
                tiles = [ox[ch * 16 + hh * 8 + half * 4 + q] for q in range(4)]
                for y in range(4):
                    line = turn(tiles[0], 32 * (0 - y))
                    for q in range(1, 4):
                        line = jnp.where(group == q, turn(tiles[q], 32 * (q - y)), line)
                    res[pl.ds((ch * 2 + half) * 64 + hh * 32 + y, 8, stride=4), :] = line
            store = pltpu.make_async_copy(
                res.at[pl.ds((ch * 2 + half) * 64, 64), :],
                result.at[ch, 0, :, pl.ds(half * 128, 128)],
                sem.at[ch * 2 + half],
            )
            store.start()
            stores.append(store)
    for store in stores:
        store.wait()


def shards(observed, intersection_strip, axial_taps, lateral_taps, extents, section_skews):
    anywhere = pl.BlockSpec(memory_space=pl.ANY)
    vmem = pl.BlockSpec(memory_space=pltpu.VMEM)
    dma = pltpu.SemaphoreType.DMA
    blocks = pl.pallas_call(
        kernel,
        out_shape=pltpu.VMEM((32, 8, 128), F32),
        in_specs=[anywhere] * 6,
        out_specs=vmem,
        scratch_shapes=[
            pltpu.SMEM((2, KZ), F32),
            pltpu.SMEM((2, KL), F32),
            pltpu.SMEM((1,), jnp.int32),
            pltpu.SMEM((1,), jnp.int32),
            dma((4,)),
            pltpu.VMEM((256, 128), F32),
            pltpu.VMEM((128, 128), F32),
            pltpu.VMEM((128, 128), F32),
            pltpu.VMEM((32, 8, 128), F32),
            pltpu.VMEM((256, 128), F32),
            pltpu.VMEM((ITERS, 8, 32, 128), F32),
            pltpu.VMEM((ITERS, 4, 8, 8, 128), F32),
            pltpu.VMEM((ITERS, 4, 16, 8, 128), F32),
            pltpu.VMEM((ITERS, 2, 4, 32, 128), F32),
            pltpu.VMEM((2, 16, 32, 128), BF16),
            pltpu.VMEM((2, 16, 32, 128), BF16),
            pltpu.VMEM((12, 32, 256), BF16),
            pltpu.VMEM((12, 32, 256), BF16),
            pltpu.VMEM((12, 32, 256), F32),
            pltpu.VMEM((1280, 512), BF16),
            pltpu.VMEM((1280, 256), BF16),
            pltpu.VMEM((32, 128), BF16),
            pltpu.VMEM((32, 128), BF16),
            pltpu.VMEM((256, 128), F32),
            dma((4,)),
            dma((4,)),
            dma((4,)),
            dma((4,)),
            dma,
            dma,
            dma((ITERS, 8)),
            dma((ITERS, 8)),
            dma,
            dma,
        ],
        compiler_params=pltpu.CompilerParams(collective_id=0, has_side_effects=True),
        name="richardson_lucy",
    )(observed, intersection_strip, axial_taps, lateral_taps, extents, section_skews)
    return pl.pallas_call(
        to_rows,
        out_shape=jax.ShapeDtypeStruct(observed.shape, F32),
        in_specs=[vmem],
        out_specs=anywhere,
        scratch_shapes=[pltpu.VMEM((256, 128), F32), dma((4,))],
        name="rows_of_blocks",
    )(pltpu.with_memory_space_constraint(blocks, pltpu.VMEM))


def solution(mesh):
    in_specs = (
        P(None, "plane", "tile", None),
        P(None, "plane", "tile", None),
        P(),
        P(),
        P("tile"),
        P("tile"),
    )
    out_specs = P(None, "plane", "tile", None)
    return jax.shard_map(shards, mesh=mesh, in_specs=in_specs, out_specs=out_specs, check_vma=False)
```

```python
import jax
import jax.numpy as jnp
from jax import lax
from jax.experimental import pallas as pl
from jax.experimental.pallas import tpu as pltpu
from jax.sharding import PartitionSpec as P

F32 = jnp.float32
BF16 = jnp.bfloat16
MESH = pl.DeviceIdType.MESH
TILES, PLANES, ITERS = 8, 32, 2
KZ, KL = 41, 15


def home_of(chan, row, xt):
    y, turn_x, q = lax.div(row, 4), lax.rem(row, 4), lax.div(xt, 2)
    px = turn_x + lax.rem(y, 2) * (3 - 2 * turn_x)
    return {"tile": 2 * y + lax.rem(xt + q, 2), "plane": 8 * px + 4 * chan + q}


def split(value):
    high = value.astype(BF16)
    return high, (value - high.astype(F32)).astype(BF16)


def lanes_of(shape):
    return lax.broadcasted_iota(jnp.int32, shape, len(shape) - 1)


def turn(value, by):
    by = by % 128
    return value if by == 0 else pltpu.roll(value, by, value.ndim - 1)


def build_lateral(taps, out, wide):
    lane = lanes_of((32, 128))
    row = lax.broadcasted_iota(jnp.int32, (32, 128), 0)
    x_lane, y_out = lane % 32, lane // 32
    x_halo = jnp.where(x_lane < 16, x_lane - 16, x_lane + 16)
    row_halo = jnp.where(row < 16, row - 16, row + 16)
    near = (x_lane >= 8) & (x_lane < 24)
    columns = 2 if wide else 1
    blocks = []
    for x_in in (row, row_halo):
        for o in range(columns):
            diff = x_in - (x_halo if o else x_lane) + 7
            if o:
                diff = jnp.where(near, diff, -1)
            block = jnp.zeros((32, 128), F32)
            for j in range(KL):
                block = jnp.where(diff == j, taps[j], block)
            blocks.append(block)
    for d in range(5):
        for y_in in range(4):
            line = jnp.zeros((32, 128), F32)
            for y in range(4):
                k = 4 * (d - 2) + y_in - y + 7
                if 0 <= k < KL:
                    line = jnp.where(y_out == y, taps[k], line)
            for b in range(2):
                rows = pl.ds((b * 640 + d * 128 if wide else d * 256 + b * 128) + y_in * 32, 32)
                for o in range(columns):
                    high, low = split(blocks[b * columns + o] * line)
                    out[rows, o * 128 : o * 128 + 128] = high
                    out[rows, (columns + o) * 128 : (columns + o) * 128 + 128] = low


def build_axial(taps, out):
    lane = lanes_of((32, 128))
    row = lax.broadcasted_iota(jnp.int32, (32, 128), 0)
    diff = lane % 32 - row + KZ // 2
    matrix = jnp.zeros((32, 128), F32)
    for j in range(KZ):
        matrix = jnp.where(diff == j, taps[j], matrix)
    high = matrix.astype(BF16).astype(F32)
    both = jnp.where(lane < 64, high, jnp.where(lane < 96, matrix - high, 0.0))
    out[...] = both.astype(BF16)


FAR_FIRST = (4, 3, 5, 2, 6, 1, 7, 0)


def kernel(
    observed, strip, axial_in, lateral_in, extents_in, skews_in, ox,
    axial, lateral, extents, skews, small_sem,
    obs_v, strip_s, strip_v, tx, rx, own, packs, hx, yh, mine, beside, qh, ql, jx, wf, wa, zf, za, ot,
    obs_sem, strip_load, strip_send, strip_recv, in_send, in_recv, halo_send, halo_recv, out_send, out_recv,
):
    t = lax.axis_index("tile")
    p = lax.axis_index("plane")
    px, pz = lax.div(p, 8), lax.rem(p, 8)
    y, core = lax.div(t, 2), lax.rem(t, 2)
    c, q_own = lax.div(pz, 4), lax.rem(pz, 4)
    xt = 2 * q_own + lax.rem(core + q_own, 2)
    rr = 4 * y + px + lax.rem(y, 2) * (3 - 2 * px)
    h = lax.rem(rr, 2)
    source = lax.div(rr, 2)
    slot = c * 16 + h * 8 + xt
    at_home = source == t

    def exists(dy, dx):
        fine = (xt + dx >= 0) & (xt + dx < 8)
        return fine & (rr + dy >= 0) & (rr + dy < 2 * TILES)

    around = [(0, -1), (0, 1)] + [(dy, dx) for dy in (-1, 1) for dx in (-1, 1)] + [(-1, 0), (1, 0)]
    homes = {(dy, dx): home_of(c, rr + dy, xt + dx) for dy, dx in around}
    there = {(dy, dx): exists(dy, dx) for dy, dx in around}
    after = {"tile": t + 1, "plane": p}
    before = {"tile": t - 1, "plane": p}

    barrier = pltpu.get_barrier_semaphore()

    def greet(to):
        pl.semaphore_signal(barrier, inc=1, device_id=to, device_id_type=MESH)

    for dz in FAR_FIRST:
        for dx in (2, 1, 3, 0):
            to = 8 * lax.rem(px + dx, 4) + lax.rem(pz + dz, 8)
            if dz + dx == 0:

                @pl.when(source != t)
                def _():
                    greet({"tile": source, "plane": to})

            else:
                greet({"tile": source, "plane": to})
    met = PLANES - jnp.where(at_home, 1, 0)
    for dy, dx in around:

        @pl.when(there[dy, dx])
        def _():
            greet(homes[dy, dx])

        met = met + jnp.where(there[dy, dx], 1, 0)

    @pl.when(t > 0)
    def _():
        greet(before)

    met = met + jnp.where(t < TILES - 1, 1, 0)

    loads = []
    strip_loads = []
    for ch in range(2):
        for half in range(2):
            i = ch * 2 + half
            lanes = pl.ds(half * 128, 128)
            strip_loads.append(
                pltpu.make_async_copy(strip.at[ch, 0, :, lanes], strip_s.at[pl.ds(i * 32, 32), :], strip_load.at[i])
            )
            loads.append(
                pltpu.make_async_copy(observed.at[ch, 0, :, lanes], obs_v.at[pl.ds(i * 64, 64), :], obs_sem.at[i])
            )
    scalar_loads = []
    for i, (src, dst) in enumerate(((axial_in, axial), (lateral_in, lateral), (extents_in, extents), (skews_in, skews))):
        scalar_loads.append(pltpu.make_async_copy(src, dst, small_sem.at[i]))
    for load in strip_loads + loads + scalar_loads:
        load.start()

    @pl.when(t == 0)
    def _():
        strip_v[...] = jnp.zeros(strip_v.shape, F32)

    for n in range(ITERS):

        @pl.when(xt == 0)
        def _():
            hx[n, 0:2] = jnp.zeros((2,) + hx.shape[2:], F32)

        @pl.when(xt == 7)
        def _():
            hx[n, 2:4] = jnp.zeros((2,) + hx.shape[2:], F32)

        for at, rows, edge_row in ((0, 0, 0), (1, 12, 2 * TILES - 1)):

            @pl.when(rr == edge_row)
            def _():
                yh[n, at] = jnp.zeros(yh.shape[2:], F32)
                hx[n, :, rows : rows + 4] = jnp.zeros((4, 4) + hx.shape[3:], F32)

    lane = lanes_of((8, 128))
    group = lane // 32

    def to_blocks(hh):
        for ch in range(2):
            for half in range(2):
                base = (ch * 2 + half) * 64 + hh * 32
                rows = [obs_v[pl.ds(base + y, 8, stride=4), :] for y in range(4)]
                for q in range(4):
                    tile = turn(rows[0], 32 * (0 - q))
                    for y in range(1, 4):
                        tile = jnp.where(group == y, turn(rows[y], 32 * (y - q)), tile)
                    tx[ch * 16 + hh * 8 + half * 4 + q] = tile

    def send_blocks(hh):
        for dz in FAR_FIRST:
            zz = lax.rem(pz + dz, 8)
            for cc in range(2):
                xx = 2 * lax.rem(zz, 4) + cc
                to = home_of(lax.div(zz, 4), 2 * t + hh, xx)

                def copy():
                    return pltpu.make_async_remote_copy(
                        src_ref=tx.at[lax.div(zz, 4) * 16 + hh * 8 + xx],
                        dst_ref=rx.at[pl.ds(pl.multiple_of(p * 8, 8), 8), :],
                        send_sem=in_send,
                        recv_sem=in_recv,
                        device_id=to,
                        device_id_type=MESH,
                    )

                if dz == 0:

                    @pl.when((to["plane"] != p) | (to["tile"] != t))
                    def _():
                        copy().start()

                else:
                    copy().start()

    for load in loads + strip_loads + scalar_loads:
        load.wait()
    to_blocks(1)
    pl.semaphore_wait(barrier, met)

    strips = []
    for i in range(4):
        rows = pl.ds(i * 32, 32)
        strips.append(
            pltpu.make_async_remote_copy(
                src_ref=strip_s.at[rows, :],
                dst_ref=strip_v.at[rows, :],
                send_sem=strip_send.at[i],
                recv_sem=strip_recv.at[i],
                device_id=after,
                device_id_type=MESH,
            )
        )

    @pl.when(t < TILES - 1)
    def _():
        for copy in strips:
            copy.start()

    send_blocks(1)

    @pl.when(t > 0)
    def _():
        for copy in strips:
            copy.wait_recv()

    reach = jnp.where(t == 0, 0, extents[0])
    skew = skews[0]
    shift = skew % 128
    wide_lane = lanes_of((32, 128))
    inside = lax.broadcasted_iota(jnp.int32, (32, 128), 0) < reach
    for ch in range(2):
        low = strip_v[pl.ds(ch * 64, 32), :]
        high = strip_v[pl.ds(ch * 64 + 32, 32), :]
        low = pltpu.roll(low, shift, 1)
        high = pltpu.roll(high, shift, 1)
        wrapped = wide_lane < shift
        first = jnp.where(wrapped, high, low)
        second = jnp.where(wrapped, low, high)
        far = skew >= 128
        for half in range(2):
            moved = jnp.where(far, (second, first)[half], (first, second)[half])
            rows = pl.ds((ch * 2 + half) * 64, 32)
            top = obs_v[rows, :]
            obs_v[rows, :] = jnp.where(inside, 0.5 * (top + moved), top)
    to_blocks(0)
    send_blocks(0)

    @pl.when(at_home)
    def _():
        rx[pl.ds(pl.multiple_of(p * 8, 8), 8), :] = tx[slot]

    lat = [lateral[c, j] for j in range(KL)]
    ax = [axial[c, j] for j in range(KZ)]
    build_axial(ax, zf)
    build_lateral(lat, wf, True)
    mine[...] = jnp.zeros(mine.shape, BF16)
    beside[...] = jnp.zeros(beside.shape, BF16)
    build_axial(ax[::-1], za)
    build_lateral(lat[::-1], wa, False)

    @pl.when(at_home)
    def _():
        most = pl.ds(0, (PLANES - 1) * 8)
        pltpu.make_async_copy(rx.at[most, :], rx.at[most, :], in_recv).wait()

    @pl.when(jnp.logical_not(at_home))
    def _():
        pltpu.make_async_copy(rx, rx, in_recv).wait()

    joined = jnp.concatenate([rx[pl.ds(ys, 32, stride=8), :][None] for ys in range(8)], axis=0)

    sent = []

    def regroup(lines):
        group = (lanes_of(lines[0].shape) // 8) % 4
        done = []
        for g in range(4):
            total = turn(lines[0], 8 * (0 - g))
            for k in range(1, 4):
                total = jnp.where(group == k, turn(lines[k], 8 * (k - g)), total)
            done.append(total)
        return done

    def banded(high, low, w, first):
        columns, rows = w.shape[1] // 2, pl.ds(first, high.shape[1])
        both = jnp.dot(high, w[rows, :], preferred_element_type=F32)
        more = jnp.dot(low, w[rows, 0:columns], preferred_element_type=F32)
        return both[:, 0:columns] + both[:, columns:] + more

    def along_z(flat, z):
        n, columns = flat.shape[0] // 32, flat.shape[1]
        high, low = split(flat.reshape(n, 32, columns))
        stacked = jnp.concatenate([high, low, high], axis=1)
        wide = jnp.concatenate([stacked[i] for i in range(n)], axis=1)
        done = jnp.dot(z[:, 0:96], wide, preferred_element_type=F32)
        return [done[:, columns * i : columns * (i + 1)] for i in range(n)]

    def padded(pad, value, first):
        pad[0, 4:12], pad[1, 4:12] = split(value)
        wide = [jnp.concatenate([pad[i, d : d + 12].reshape(384, 128) for d in range(5)], axis=1) for i in range(2)]
        return banded(wide[0], wide[1], wf, first)

    def beyond(value, at, first):
        wide = []
        for part in split(value):
            none = jnp.zeros((32, 128), BF16)
            columns = []
            for d in range(4):
                lines = [i + d if at == 0 else i + d - 3 for i in range(4)]
                columns.append(jnp.concatenate([part[i] if 0 <= i < 4 else none for i in lines], axis=0))
            wide.append(jnp.concatenate(columns, axis=1))
        return banded(wide[0], wide[1], wf, first + 128 * at)

    def forward(value, n):
        own[n] = value
        for g, pack in enumerate(regroup([value[:, 8 * k : 8 * k + 8, :] for k in range(4)])):
            packs[n, g] = pack
        copies = {}
        for i, (dy, dx) in enumerate(around):
            rows, size, at = {-1: (0, 4, 12), 0: (0, 8, 4), 1: (4, 4, 0)}[dy]
            if dx == 0:
                src, dst = own.at[n, pl.ds(rows, 4)], yh.at[n, 0 if dy == 1 else 1]
            else:
                side = (2, 0) if dx == 1 else (0, 2)
                src = packs.at[n, pl.ds(side[0], 2), pl.ds(rows, size)]
                dst = hx.at[n, pl.ds(side[1], 2), pl.ds(at, size)]
            copy = pltpu.make_async_remote_copy(
                src_ref=src,
                dst_ref=dst,
                send_sem=halo_send.at[n, i],
                recv_sem=halo_recv.at[n, i],
                device_id=homes[dy, dx],
                device_id_type=MESH,
            )
            copies[dy, dx] = copy

            @pl.when(there[dy, dx])
            def _():
                copy.start()

            sent.append((there[dy, dx], copy))
        def arrive(which):
            for dy, dx in around:
                if which(dy, dx):

                    @pl.when(there[-dy, -dx])
                    def _():
                        copies[dy, dx].wait_recv()

        blurred = along_z(padded(mine, value, 0), zf)
        arrive(lambda dy, dx: dy == 0)
        sides = jnp.concatenate(regroup([hx[n, g, 4:12] for g in range(4)]), axis=1)
        side = padded(beside, sides, 640)
        arrive(lambda dy, dx: dy * dx != 0)
        corner = [jnp.concatenate(regroup([hx[n, g, r : r + 4] for g in range(4)]), axis=1) for r in (0, 12)]
        diagonal = [beyond(corner[at], at, 640) for at in range(2)]
        arrive(lambda dy, dx: dx == 0)
        straight = [beyond(yh[n, at], at, 0) for at in range(2)]
        outer = []
        for at in range(2):
            corners = corner[at]
            outer.append(straight[at] + diagonal[at])
            if n == 0:
                edge, near = ((0, 2), (2, 4)) if at == 0 else ((10, 12), (0, 2))
                jx[edge[0] : edge[1], :, 0:128] = yh[n, at, near[0] : near[1]]
                jx[edge[0] : edge[1], :, 128:256] = corners[near[0] : near[1]]
        if n == 0:
            jx[2:10, :, 0:128] = value
            jx[2:10, :, 128:256] = sides
        rest = jnp.concatenate([side[0:128] + outer[0], side[128:256], side[256:384] + outer[1]], axis=0)
        blurred = [a + b for a, b in zip(blurred, along_z(rest, zf))]
        return blurred

    def shifts(lines, size):
        return jnp.concatenate([lines[d : d + size].reshape(size * 32, 256) for d in range(5)], axis=1)

    wide_lane = lanes_of((32, 256))
    near = (wide_lane // 8) % 4
    on_slab = (wide_lane < 128) | ((near == 1) & (xt > 0)) | ((near == 2) & (xt < 7))
    estimate = joined
    for sweep in range(ITERS):
        blurred = forward(estimate, sweep)
        for i in range(12):
            inside = on_slab
            if i < 2:
                inside = inside & (rr > 0)
            if i >= 10:
                inside = inside & (rr < 2 * TILES - 1)
            qh[i], ql[i] = split(jnp.where(inside, jx[i] / blurred[i], 0.0))
        factor = along_z(banded(shifts(qh, 8), shifts(ql, 8), wa, 0), za)
        estimate = estimate * jnp.concatenate([line[None] for line in factor], axis=0)

    for ys in range(8):
        ot[pl.ds(ys, 32, stride=8), :] = estimate[ys]

    for dz in FAR_FIRST:
        zz = lax.rem(pz + dz, 8)
        for dx in (2, 1, 3, 0):
            to = 8 * lax.rem(px + dx, 4) + zz

            def copy():
                return pltpu.make_async_remote_copy(
                    src_ref=ot.at[pl.ds(pl.multiple_of(to * 8, 8), 8), :],
                    dst_ref=ox.at[slot],
                    send_sem=out_send,
                    recv_sem=out_recv,
                    device_id={"tile": source, "plane": to},
                    device_id_type=MESH,
                )

            if dz + dx == 0:

                @pl.when(jnp.logical_not(at_home))
                def _():
                    copy().start()

            else:
                copy().start()

    @pl.when(at_home)
    def _():
        ox[slot] = ot[pl.ds(pl.multiple_of(p * 8, 8), 8), :]

    @pl.when(t < TILES - 1)
    def _():
        for copy in strips:
            copy.wait_send()

    for used, copy in sent:

        @pl.when(used)
        def _():
            copy.wait_send()

    @pl.when(at_home)
    def _():
        few = pl.ds(0, PLANES - 1)
        pltpu.make_async_copy(tx.at[few], tx.at[few], in_send).wait()
        pltpu.make_async_copy(ox.at[few], ox.at[few], out_recv).wait()
        pltpu.make_async_copy(ox.at[few], ox.at[few], out_send).wait()

    @pl.when(jnp.logical_not(at_home))
    def _():
        pltpu.make_async_copy(tx, tx, in_send).wait()
        pltpu.make_async_copy(ox, ox, out_recv).wait()
        pltpu.make_async_copy(ox, ox, out_send).wait()


def to_rows(ox, result, res, sem):
    group = lanes_of((8, 128)) // 32
    stores = []
    for ch in range(2):
        for half in range(2):
            for hh in range(2):
                tiles = [ox[ch * 16 + hh * 8 + half * 4 + q] for q in range(4)]
                for y in range(4):
                    line = turn(tiles[0], 32 * (0 - y))
                    for q in range(1, 4):
                        line = jnp.where(group == q, turn(tiles[q], 32 * (q - y)), line)
                    res[pl.ds((ch * 2 + half) * 64 + hh * 32 + y, 8, stride=4), :] = line
            store = pltpu.make_async_copy(
                res.at[pl.ds((ch * 2 + half) * 64, 64), :],
                result.at[ch, 0, :, pl.ds(half * 128, 128)],
                sem.at[ch * 2 + half],
            )
            store.start()
            stores.append(store)
    for store in stores:
        store.wait()


def shards(observed, intersection_strip, axial_taps, lateral_taps, extents, section_skews):
    anywhere = pl.BlockSpec(memory_space=pl.ANY)
    vmem = pl.BlockSpec(memory_space=pltpu.VMEM)
    dma = pltpu.SemaphoreType.DMA
    blocks = pl.pallas_call(
        kernel,
        out_shape=pltpu.VMEM((32, 8, 128), F32),
        in_specs=[anywhere] * 6,
        out_specs=vmem,
        scratch_shapes=[
            pltpu.SMEM((2, KZ), F32),
            pltpu.SMEM((2, KL), F32),
            pltpu.SMEM((1,), jnp.int32),
            pltpu.SMEM((1,), jnp.int32),
            dma((4,)),
            pltpu.VMEM((256, 128), F32),
            pltpu.VMEM((128, 128), F32),
            pltpu.VMEM((128, 128), F32),
            pltpu.VMEM((32, 8, 128), F32),
            pltpu.VMEM((256, 128), F32),
            pltpu.VMEM((ITERS, 8, 32, 128), F32),
            pltpu.VMEM((ITERS, 4, 8, 8, 128), F32),
            pltpu.VMEM((ITERS, 4, 16, 8, 128), F32),
            pltpu.VMEM((ITERS, 2, 4, 32, 128), F32),
            pltpu.VMEM((2, 16, 32, 128), BF16),
            pltpu.VMEM((2, 16, 32, 128), BF16),
            pltpu.VMEM((12, 32, 256), BF16),
            pltpu.VMEM((12, 32, 256), BF16),
            pltpu.VMEM((12, 32, 256), F32),
            pltpu.VMEM((1280, 512), BF16),
            pltpu.VMEM((1280, 256), BF16),
            pltpu.VMEM((32, 128), BF16),
            pltpu.VMEM((32, 128), BF16),
            pltpu.VMEM((256, 128), F32),
            dma((4,)),
            dma((4,)),
            dma((4,)),
            dma((4,)),
            dma,
            dma,
            dma((ITERS, 8)),
            dma((ITERS, 8)),
            dma,
            dma,
        ],
        compiler_params=pltpu.CompilerParams(collective_id=0, has_side_effects=True),
        name="richardson_lucy",
    )(observed, intersection_strip, axial_taps, lateral_taps, extents, section_skews)
    return pl.pallas_call(
        to_rows,
        out_shape=jax.ShapeDtypeStruct(observed.shape, F32),
        in_specs=[vmem],
        out_specs=anywhere,
        scratch_shapes=[pltpu.VMEM((256, 128), F32), dma((4,))],
        name="rows_of_blocks",
    )(pltpu.with_memory_space_constraint(blocks, pltpu.VMEM))


def solution(mesh):
    in_specs = (
        P(None, "plane", "tile", None),
        P(None, "plane", "tile", None),
        P(),
        P(),
        P("tile"),
        P("tile"),
    )
    out_specs = P(None, "plane", "tile", None)
    return jax.shard_map(shards, mesh=mesh, in_specs=in_specs, out_specs=out_specs, check_vma=False)
```
